128 devices in a mesh: lat: 16 (over z, x_hi, core), lon: 8 (over y, x_lo).
Axes of the slice: x: 4 (x_hi: 2, x_lo: 2; x = x_hi * 2 + x_lo), y: 4, z: 4, core: 2. Of those that a mesh axis runs over, the one named last changes fastest.
Arguments:
- thermal_anomaly: float32 [40, 128, 12288], P(None, 'lat', 'lon'), may hold values from -6 to 6
- saltiness_anomaly: float32 [40, 128, 12288], P(None, 'lat', 'lon'), may hold values from -6 to 6
- easterly_flow: float32 [40, 128, 12288], P(None, 'lat', 'lon'), may hold values from -3 to 3
- poleward_flow: float32 [40, 128, 12288], P(None, 'lat', 'lon'), may hold values from -3 to 3
- planetary_spin: float32 [128], P('lat'), may hold values from -1.5 to 1.5
- marine_indicator: int32 [40, 128, 12288], P(None, 'lat', 'lon'), may hold values 0 or 1
- active_strata: int32 [128, 12288], P('lat', 'lon'), may hold values from 1 to 40
Outputs:
- temperature_next: float32 [40, 128, 12288], P(None, 'lat', 'lon')
- salinity_next: float32 [40, 128, 12288], P(None, 'lat', 'lon')
- easterly_flow_after: float32 [40, 128, 12288], P(None, 'lat', 'lon')
- meridional_next: float32 [40, 128, 12288], P(None, 'lat', 'lon')
- spectral_capture: bfloat16 [2, 10, 32, 3072], P(None, None, 'lat')
The draws below stay inside these ranges and needn't reach their ends.
All inputs are finite; a program needn't handle non-finite values. No bound on the sum of `marine_indicator` on one device may be relied on, other than what follows from the above.
Results may differ from the reference program's by a relative error of at most 0.003.
Values may be sent and summed in bfloat16 or wider, within the bound.
A program may use at most 192 MiB of HBM per device.

```python
import math
import jax
import jax.numpy as jnp
from jax import lax

STRATUM_COUNT = 40
PARALLEL_COUNT = 128
MERIDIAN_COUNT = 12288


def touch_ends(result, stream_key, low, high):
    extent = result.shape
    spot = [jax.random.randint(jax.random.fold_in(stream_key, axis), (), 0, extent[axis]) for axis in range(len(extent))]
    result = result.at[tuple(spot)].set(low)
    longest = extent.index(max(extent))
    spot[longest] = (spot[longest] + 1) % extent[longest]
    return result.at[tuple(spot)].set(high)


def shard_levels(own_key, shape, cuts, least, high):
    loudness = 1.0
    for dim, shards_of in cuts:
        draws = jax.random.uniform(jax.random.fold_in(jax.random.fold_in(own_key, 6), dim), (shards_of,), jnp.float32, least / len(cuts), high / len(cuts))
        loudness = loudness * jnp.repeat(jnp.exp(draws), shape[dim] // shards_of).reshape((-1,) + (1,) * (len(shape) - 1 - dim))
    return loudness


def noise(stream_key, shape, scale, limit, shards=(), dtype=jnp.bfloat16):
    result = jax.random.normal(stream_key, shape, jnp.float32) * scale
    if len(shards) > 0:
        result = shard_levels(stream_key, shape, shards, -0.22, 0.18) * result
    return jnp.clip(result, min=-limit, max=limit).astype(dtype)


def setup_inputs(seed: int = 0) -> dict:
    key_list = jax.random.split(jax.random.key(seed), 8)
    thermal_anomaly = noise(key_list[0], (STRATUM_COUNT, PARALLEL_COUNT, MERIDIAN_COUNT), 1.0, 6.0, ((1, 16), (2, 8)), jnp.float32)
    saltiness_anomaly = noise(key_list[1], (STRATUM_COUNT, PARALLEL_COUNT, MERIDIAN_COUNT), 1.0, 6.0, ((1, 16), (2, 8)), jnp.float32)
    easterly_flow = noise(key_list[2], (STRATUM_COUNT, PARALLEL_COUNT, MERIDIAN_COUNT), 0.5, 3.0, ((1, 16), (2, 8)), jnp.float32)
    poleward_flow = noise(key_list[3], (STRATUM_COUNT, PARALLEL_COUNT, MERIDIAN_COUNT), 0.5, 3.0, ((1, 16), (2, 8)), jnp.float32)
    planetary_spin = jnp.clip(jax.random.uniform(key_list[4], (PARALLEL_COUNT,), jnp.float32, -1.5, 1.5) * shard_levels(key_list[4], (PARALLEL_COUNT,), ((0, 16),), -0.4, 0.0), -1.5, 1.5)
    marine_indicator = touch_ends((jax.random.randint(key_list[5], (STRATUM_COUNT, PARALLEL_COUNT, MERIDIAN_COUNT), 0, 8) < 7).astype(jnp.int32), jax.random.fold_in(key_list[5], 1), 0, 1)
    active_strata = touch_ends(jax.random.randint(key_list[6], (PARALLEL_COUNT, MERIDIAN_COUNT), 1, STRATUM_COUNT + 1), jax.random.fold_in(key_list[6], 1), 1, STRATUM_COUNT).astype(jnp.int32)
    return dict(thermal_anomaly=thermal_anomaly, saltiness_anomaly=saltiness_anomaly, easterly_flow=easterly_flow, poleward_flow=poleward_flow, planetary_spin=planetary_spin, marine_indicator=marine_indicator, active_strata=active_strata)


ENLARGE_RATIO = 0.2
REDUCE_RATIO = 0.8
PRESSURE_SCALE = 0.25
TIME_STEP = 0.5
COURANT = 0.2
LATERAL_MIXING = 0.8
VERTICAL_MIXING = 0.1

def wet_cells(marine_indicator, active_strata):
    depth_index = lax.broadcasted_iota(jnp.int32, marine_indicator.shape, 0)
    active = (depth_index < active_strata[None, :, :]).astype(jnp.int32)
    return (marine_indicator * active).astype(jnp.float32)

def evaluate_stress_head(thermal_anomaly, saltiness_anomaly, marine_share):
    seawater_heaviness = marine_share * (REDUCE_RATIO * saltiness_anomaly - ENLARGE_RATIO * thermal_anomaly)
    return PRESSURE_SCALE * (jnp.cumsum(seawater_heaviness, axis=0) - 0.5 * seawater_heaviness)

def momentum(zonal, merid, marine_share, planetary_spin, weight_column_stress):
    press_dx = weight_column_stress[:, 1:-1, 2:] - weight_column_stress[:, 1:-1, :-2]
    press_dy = weight_column_stress[:, 2:, 1:-1] - weight_column_stress[:, :-2, 1:-1]
    rotation = planetary_spin[:, None]
    easterly_flow_after = marine_share * (zonal + TIME_STEP * (rotation * merid - 0.5 * press_dx))
    poleward_flow_after = marine_share * (merid + TIME_STEP * (-rotation * zonal - 0.5 * press_dy))
    return (easterly_flow_after, poleward_flow_after)

def march_scalar_field(tracer, marine_share, zonal, merid):
    row_tracer = tracer[:, 1:-1, :]
    row_wet = marine_share[:, 1:-1, :]
    row_zonal = zonal[:, 1:-1, :]
    east_flux = row_wet[:, :, :-1] * row_wet[:, :, 1:] * (0.25 * (row_zonal[:, :, :-1] + row_zonal[:, :, 1:]) * (row_tracer[:, :, :-1] + row_tracer[:, :, 1:]) - LATERAL_MIXING * (row_tracer[:, :, 1:] - row_tracer[:, :, :-1]))
    col_tracer = tracer[:, :, 1:-1]
    col_wet = marine_share[:, :, 1:-1]
    col_merid = merid[:, :, 1:-1]
    north_flux = col_wet[:, :-1, :] * col_wet[:, 1:, :] * (0.25 * (col_merid[:, :-1, :] + col_merid[:, 1:, :]) * (col_tracer[:, :-1, :] + col_tracer[:, 1:, :]) - LATERAL_MIXING * (col_tracer[:, 1:, :] - col_tracer[:, :-1, :]))
    center = tracer[:, 1:-1, 1:-1]
    wet_center = marine_share[:, 1:-1, 1:-1]
    vertical = wet_center[:-1] * wet_center[1:] * (-VERTICAL_MIXING * (center[1:] - center[:-1]))
    zero_plane = jnp.zeros_like(center[:1])
    vertical = jnp.concatenate([zero_plane, vertical, zero_plane], axis=0)
    return wet_center * (center - COURANT * (east_flux[:, :, 1:] - east_flux[:, :, :-1]) - COURANT * (north_flux[:, 1:, :] - north_flux[:, :-1, :]) - (vertical[1:] - vertical[:-1]))

def enlarge_everywhere(field, width):
    padded = jnp.pad(field, ((0, 0), (width, width), (0, 0)))
    return jnp.pad(padded, ((0, 0), (0, 0), (width, width)), mode='wrap')

def dct_table():
    freq = lax.broadcasted_iota(jnp.int32, (2, 8), 0).astype(jnp.float32)
    place = lax.broadcasted_iota(jnp.int32, (2, 8), 1).astype(jnp.float32)
    scale = jnp.where(freq > 0.5, math.sqrt(2.0 / 8.0), math.sqrt(1.0 / 8.0))
    return scale * jnp.cos(math.pi * (2.0 * place + 1.0) * freq / 16.0)

def condense_spectrum(field):
    table = dct_table()
    high = lax.Precision.HIGHEST
    blocks = field.reshape(STRATUM_COUNT // 8, 8, PARALLEL_COUNT // 8, 8, MERIDIAN_COUNT // 8, 8)
    blocks = jnp.einsum('anbmcl,rl->anbmcr', blocks, table, precision=high)
    blocks = jnp.einsum('anbmcr,qm->anbqcr', blocks, table, precision=high)
    blocks = jnp.einsum('anbqcr,pn->apbqcr', blocks, table, precision=high)
    return blocks.reshape(STRATUM_COUNT // 4, PARALLEL_COUNT // 4, MERIDIAN_COUNT // 4)

def reference(thermal_anomaly, saltiness_anomaly, easterly_flow, poleward_flow, planetary_spin, marine_indicator, active_strata):
    marine_share = wet_cells(marine_indicator, active_strata)
    weight_column_stress = evaluate_stress_head(thermal_anomaly, saltiness_anomaly, marine_share)
    easterly_flow_after, poleward_flow_after = momentum(easterly_flow, poleward_flow, marine_share, planetary_spin, enlarge_everywhere(weight_column_stress, 1))
    marine_sweep = enlarge_everywhere(marine_share, 1)
    easterly_sweep = enlarge_everywhere(easterly_flow_after, 1)
    poleward_sweep = enlarge_everywhere(poleward_flow_after, 1)
    thermal_after = march_scalar_field(enlarge_everywhere(thermal_anomaly, 1), marine_sweep, easterly_sweep, poleward_sweep)
    brine_following = march_scalar_field(enlarge_everywhere(saltiness_anomaly, 1), marine_sweep, easterly_sweep, poleward_sweep)
    spectral_capture = jnp.stack([condense_spectrum(thermal_after), condense_spectrum(brine_following)]).astype(jnp.bfloat16)
    return (thermal_after, brine_following, easterly_flow_after, poleward_flow_after, spectral_capture)
```

```python
import functools
import math

import jax
import jax.numpy as jnp
from jax import lax
from jax.experimental import pallas as pl
from jax.experimental.pallas import tpu as pltpu
from jax.sharding import PartitionSpec as P

MESH = pl.DeviceIdType.MESH
BUOY_SALT = 0.25 * 0.25 * 0.8
BUOY_HEAT = 0.25 * 0.25 * 0.2
CARRY = 0.2 * 0.25
MIX = 0.2 * 0.8
VERT = 0.1
FLAT = math.sqrt(1.0 / 8.0)
WAVE = [math.sqrt(2.0 / 8.0) * math.cos(math.pi * (2 * n + 1) / 16.0) for n in range(8)]
ROWS = 8
LANES = 128
BLOCK = 8


def pairwise_sum(parts):
    while len(parts) > 1:
        parts = [sum(parts[i : i + 2][1:], parts[i]) for i in range(0, len(parts), 2)]
    return parts[0]


def table_value(freq, place):
    wave = jnp.full(freq.shape, WAVE[0], jnp.float32)
    for n in range(1, 8):
        wave = jnp.where(place == n, WAVE[n], wave)
    return jnp.where(freq == 0, FLAT, wave)


def fluxes(near, far, both, pairs):
    t = CARRY * (near + far)
    a = both * (t + MIX)
    b = both * (t - MIX)
    return [a * q + b * n for q, n in pairs]


def step_kernel(
    n_lat,
    n_lon,
    spin,
    heat_hbm,
    salt_hbm,
    east_hbm,
    pole_hbm,
    sea_hbm,
    depth_hbm,
    heat_out,
    salt_out,
    east_out,
    pole_out,
    coef_out,
    heat,
    salt,
    east,
    pole,
    sea,
    depth,
    wet,
    press,
    row_send,
    from_south,
    from_north,
    edge_box,
    side_send,
    from_west,
    from_east,
    halo_box,
    halo_cols,
    upward,
    tower,
    lane_table,
    row_table,
    stack,
    coef_send,
    load_sem,
    depth_sem,
    row_send_sem,
    south_sem,
    north_sem,
    side_send_sem,
    west_sem,
    east_sem,
    coef_send_sem,
    coef_sem,
):
    chunks = depth.shape[0] // ROWS
    cols = chunks * LANES
    tall = chunks * ROWS
    total = press.shape[0]
    blocks = total // (tall * BLOCK)
    slab = BLOCK * ROWS
    la = lax.axis_index("lat")
    lo = lax.axis_index("lon")
    above = {"lat": lax.rem(la + 1, n_lat)}
    below = {"lat": lax.rem(la + n_lat - 1, n_lat)}
    right = {"lon": lax.rem(lo + 1, n_lon)}
    left = {"lon": lax.rem(lo + n_lon - 1, n_lon)}
    has_above = la < n_lat - 1
    has_below = la > 0

    fields = ((heat_hbm, heat), (salt_hbm, salt), (sea_hbm, sea), (east_hbm, east), (pole_hbm, pole))

    def load(i, b):
        hbm, vmem = fields[i]
        part = pl.ds(pl.multiple_of(b * BLOCK * tall, BLOCK * tall), BLOCK * tall)
        return pltpu.make_async_copy(hbm.at[part], vmem.at[part], load_sem.at[i, b])

    depth_load = pltpu.make_async_copy(depth_hbm, depth, depth_sem)
    depth_load.start()
    for b in range(blocks):
        for i in range(len(fields)):
            load(i, b).start()

    barrier = pltpu.get_barrier_semaphore()
    peers = [above, below] + [{"lon": lax.rem(lo + d, n_lon)} for d in range(1, n_lon)]
    for peer in peers:
        pl.semaphore_signal(barrier, inc=1, device_id=peer, device_id_type=MESH)

    lane = lax.broadcasted_iota(jnp.int32, (ROWS, LANES), 1)
    row = lax.broadcasted_iota(jnp.int32, (ROWS, LANES), 0)
    spin_half = jnp.full((ROWS, LANES), 0.5 * spin[0], jnp.float32)
    for j in range(1, ROWS):
        spin_half = jnp.where(row == j, 0.5 * spin[j], spin_half)
    zero = jnp.zeros((ROWS, LANES), jnp.float32)

    deep, wide = lane_table.shape
    n = lax.broadcasted_iota(jnp.int32, (deep, wide), 0)
    o = lax.broadcasted_iota(jnp.int32, (deep, wide), 1)
    lane_table[...] = jnp.where(n // 8 == o // 2, table_value(o % 2, n % 8), 0.0)
    n = lax.broadcasted_iota(jnp.int32, row_table.shape, 1)
    o = lax.broadcasted_iota(jnp.int32, row_table.shape, 0)
    row_table[...] = jnp.where(n // 8 == o // 2, table_value(o % 2, n % 8), 0.0)
    edge_box[...] = jnp.zeros_like(edge_box)
    halo_box[...] = jnp.zeros_like(halo_box)
    upward[...] = jnp.zeros_like(upward)
    tower[...] = jnp.zeros_like(tower)
    for f in (heat, salt, wet):
        f[total:, :] = jnp.zeros((tall, LANES), jnp.float32)

    @pl.when(la == 0)
    def _():
        from_south[...] = jnp.zeros_like(from_south)

    @pl.when(la == n_lat - 1)
    def _():
        from_north[...] = jnp.zeros_like(from_north)

    depth_load.wait()
    pl.semaphore_wait(barrier, len(peers))

    def at(k, c):
        return pl.ds(pl.multiple_of(k * tall, tall) + c * ROWS, ROWS)

    def lines(b, j, c):
        return pl.ds(pl.multiple_of(b * BLOCK * tall, BLOCK * tall) + (c * ROWS + j), BLOCK, stride=tall)

    def row_copy(b, side):
        return pltpu.make_async_remote_copy(
            src_ref=row_send.at[side, b],
            dst_ref=(from_north if side == 0 else from_south).at[b],
            send_sem=row_send_sem.at[side, b],
            recv_sem=(north_sem if side == 0 else south_sem).at[b],
            device_id=below if side == 0 else above,
            device_id_type=MESH,
        )

    def side_copy(b, side):
        return pltpu.make_async_remote_copy(
            src_ref=side_send.at[b],
            dst_ref=(from_east if side == 0 else from_west).at[b],
            send_sem=side_send_sem.at[side, b],
            recv_sem=(east_sem if side == 0 else west_sem).at[b],
            device_id=left if side == 0 else right,
            device_id_type=MESH,
        )

    def coef_copy(b, d):
        place = pl.ds(pl.multiple_of(lo * (cols // 4), LANES), cols // 4)
        return pltpu.make_async_remote_copy(
            src_ref=coef_send.at[b],
            dst_ref=coef_out.at[:, pl.ds(2 * b, 2), :, place],
            send_sem=coef_send_sem.at[b, d],
            recv_sem=coef_sem.at[b, d],
            device_id={"lon": lax.rem(lo + d, n_lon)},
            device_id_type=MESH,
        )

    def first(b, running):
        for i in range(len(fields)):
            load(i, b).wait()

        def level(i, running):
            k = b * BLOCK + i
            out = []
            for c in range(chunks):
                here = at(k, c)
                w = jnp.where(k < depth[c * ROWS : (c + 1) * ROWS, :], sea[here, :], 0).astype(jnp.float32)
                d = w * (BUOY_SALT * salt[here, :] - BUOY_HEAT * heat[here, :])
                s = running[c] + d
                wet[here, :] = w
                press[here, :] = s - 0.5 * d
                out.append(s)
            return tuple(out)

        running = lax.fori_loop(0, BLOCK, level, running)

        for i in range(BLOCK):
            for side in range(2):
                here = at(b * BLOCK + i, 0 if side == 0 else chunks - 1)
                p = press[here, :]
                w = wet[here, :]
                flow = east[here, :] + spin_half * pole[here, :]
                if side == 0:
                    part = w * (flow - pltpu.roll(p, LANES - 1, 1))
                else:
                    part = w * (flow + pltpu.roll(p, 1, 1))
                box = zero
                for f, v in enumerate((heat[here, :], salt[here, :], w, part, p)):
                    shift = f if side == 0 else f + 1
                    v = pltpu.roll(v, shift, 1) if shift else v
                    box = jnp.where(lane == f, v, box)
                edge_box[side * slab + i * ROWS : side * slab + (i + 1) * ROWS, :] = box
        side_send[b] = edge_box[...].T[:ROWS, :]
        side_copy(b, 0).start()
        side_copy(b, 1).start()

        for side in range(2):
            j, inner = (0, 1) if side == 0 else (ROWS - 1, ROWS - 2)
            f = 0.5 * spin[j]
            for c in range(chunks):
                ch = slice(c * LANES, (c + 1) * LANES)

                def line(ref, j):
                    return ref[lines(b, j, c), :]

                w = line(wet, j)
                p = line(press, inner)
                flow = line(pole, j) - f * line(east, j)
                part = w * (flow - p) if side == 0 else w * (flow + p)
                row_send[side, b, 0:16, ch] = jnp.concatenate([line(heat, j), line(salt, j)], 0).astype(jnp.bfloat16)
                row_send[side, b, 16:32, ch] = jnp.concatenate([w, part], 0).astype(jnp.bfloat16)

        @pl.when(has_below)
        def _():
            row_copy(b, 0).start()

        @pl.when(has_above)
        def _():
            row_copy(b, 1).start()

        return running

    lax.fori_loop(0, blocks, first, (zero,) * chunks)

    def second(b, _):
        side_copy(b, 0).wait_recv()
        side_copy(b, 1).wait_recv()
        halo_box[0:ROWS, :] = jnp.where(lane < slab, from_east[b], from_west[b])
        halo_cols[...] = halo_box[...].T

        def level(i, _):
            k = b * BLOCK + i
            over_east = halo_cols[pl.ds(pl.multiple_of(i * ROWS, ROWS), ROWS), :]
            over_west = halo_cols[pl.ds(pl.multiple_of(slab + i * ROWS, ROWS), ROWS), :]
            last = LANES - 1

            def chunk(ref, c):
                return ref[at(k, c), :]

            def to_last(f):
                return pltpu.roll(over_east, last - f, 1)

            def to_first(f):
                return pltpu.roll(over_west, LANES - f, 1) if f else over_west

            def ahead(turned, c):
                return jnp.where(lane == last, turned[c + 1], turned[c])

            p = [chunk(press, c) for c in range(chunks)]
            w = [chunk(wet, c) for c in range(chunks)]
            p_ahead = [pltpu.roll(x, last, 1) for x in p] + [to_last(4)]
            p_back = [to_first(4)] + [pltpu.roll(x, 1, 1) for x in p]
            u, v = [], []
            for c in range(chunks):
                e, n = chunk(east, c), chunk(pole, c)
                dx = ahead(p_ahead, c) - jnp.where(lane == 0, p_back[c], p_back[c + 1])
                u.append(w[c] * (e + (spin_half * n - dx)))
                north = jnp.where(row == ROWS - 1, 0.0, pltpu.roll(p[c], ROWS - 1, 0))
                south = jnp.where(row == 0, 0.0, pltpu.roll(p[c], 1, 0))
                v.append(w[c] * (n - (spin_half * e + (north - south))))
                east_out[at(k, c), :] = u[c]
                pole_out[at(k, c), :] = v[c]

            q = [[chunk(f, c) for c in range(chunks)] for f in (heat, salt)]
            w_ahead = [pltpu.roll(x, last, 1) for x in w] + [to_last(2)]
            u_ahead = [pltpu.roll(x, last, 1) for x in u]
            u_ahead.append(to_last(3) + to_last(2) * p[chunks - 1])
            q_ahead = [
                [pltpu.roll(x, last, 1) for x in q[t]] + [to_last(t)] for t in range(2)
            ]
            w_out = to_first(2)
            u_out = to_first(3) - w_out * p[0]
            flux_back = fluxes(
                u_out, u[0], w_out * w[0], [(to_first(t), q[t][0]) for t in range(2)]
            )
            for c in range(chunks):
                flux = fluxes(
                    u[c],
                    ahead(u_ahead, c),
                    w[c] * ahead(w_ahead, c),
                    [(q[t][c], ahead(q_ahead[t], c)) for t in range(2)],
                )
                turned = [pltpu.roll(x, 1, 1) for x in flux]
                flux_n = fluxes(
                    v[c],
                    pltpu.roll(v[c], ROWS - 1, 0),
                    w[c] * jnp.where(row == ROWS - 1, 0.0, pltpu.roll(w[c], ROWS - 1, 0)),
                    [(q[t][c], pltpu.roll(q[t][c], ROWS - 1, 0)) for t in range(2)],
                )
                both = VERT * (w[c] * wet[at(k + 1, c), :])
                for t, (f, out) in enumerate(((heat, heat_out), (salt, salt_out))):
                    above_q = f[at(k + 1, c), :]
                    rise = both * (above_q - q[t][c])
                    held = slice((t * chunks + c) * ROWS, (t * chunks + c + 1) * ROWS)
                    gain = rise - upward[held, :]
                    upward[held, :] = rise
                    dx = flux[t] - jnp.where(lane == 0, flux_back[t], turned[t])
                    dy = flux_n[t] - pltpu.roll(flux_n[t], 1, 0)
                    out[at(k, c), :] = w[c] * ((q[t][c] + gain) - (dx + dy))
                flux_back = turned
            return 0

        lax.fori_loop(0, BLOCK, level, 0)
        return 0

    lax.fori_loop(0, blocks, second, 0)

    def third(b, _):
        for side in range(2):
            got = from_north if side == 0 else from_south
            j, inner = (ROWS - 1, ROWS - 2) if side == 0 else (0, 1)

            @pl.when(has_above if side == 0 else has_below)
            def _():
                row_copy(b, side).wait_recv()

            for c in range(chunks):
                ch = slice(c * LANES, (c + 1) * LANES)

                def line(ref, j):
                    return ref[lines(b, j, c), :]

                tracers = got[b, 0:16, ch].astype(jnp.float32)
                rest = got[b, 16:32, ch].astype(jnp.float32)
                q_far = (tracers[0:8], tracers[8:16])
                w_far, v_far = rest[0:8], rest[8:16]
                d = w_far * (BUOY_SALT * q_far[1] - BUOY_HEAT * q_far[0])
                s = d
                for gap in (1, 2, 4):
                    s = s + jnp.where(row >= gap, pltpu.roll(s, gap, 0), 0.0)
                held = slice((side * chunks + c) * ROWS, (side * chunks + c + 1) * ROWS)
                s = s + tower[held, :]
                tower[held, :] = jnp.broadcast_to(s[BLOCK - 1 : BLOCK, :], (BLOCK, LANES))
                p_far = s - 0.5 * d
                w, w_in = line(wet, j), line(wet, inner)
                p = line(press, j)
                if side == 0:
                    change = -(w * p_far)
                    v_far = v_far + w_far * p
                else:
                    change = w * p_far
                    v_far = v_far - w_far * p
                v = line(pole_out, j) + change
                pole_out[lines(b, j, c), :] = v
                t = CARRY * (v + v_far)
                both = w * w_far
                up = both * (t + MIX)
                down = both * (t - MIX)
                inside = (w * w_in) * (CARRY * change)
                for f, out, far in ((heat, heat_out, q_far[0]), (salt, salt_out, q_far[1])):
                    q, q_in = line(f, j), line(f, inner)
                    shift = inside * (q + q_in)
                    if side == 0:
                        edge = shift - (up * q + down * far)
                        back = -shift
                    else:
                        edge = (up * far + down * q) - shift
                        back = shift
                    out[lines(b, j, c), :] = line(out, j) + edge
                    out[lines(b, inner, c), :] = line(out, inner) + back

        groups = chunks // 4
        for t, f in enumerate((heat_out, salt_out)):
            for c in range(chunks):
                x = [f[at(b * BLOCK + i, c), :] for i in range(BLOCK)]
                add = [x[i] + x[BLOCK - 1 - i] for i in range(BLOCK // 2)]
                dif = [WAVE[i] * (x[i] - x[BLOCK - 1 - i]) for i in range(BLOCK // 2)]
                g, s = c // 4, slice((c % 4) * LANES, (c % 4 + 1) * LANES)
                base = g * 4 * ROWS + t * 2 * ROWS
                stack[base : base + ROWS, s] = FLAT * pairwise_sum(add)
                stack[base + ROWS : base + 2 * ROWS, s] = pairwise_sum(dif)
        short = jnp.dot(
            stack[...], lane_table[...], precision=lax.Precision.HIGHEST, preferred_element_type=jnp.float32
        )
        for g in range(groups):
            done = jnp.dot(
                row_table[...],
                short[g * 4 * ROWS : (g + 1) * 4 * ROWS, :],
                precision=lax.Precision.HIGHEST,
                preferred_element_type=jnp.float32,
            )
            for t in range(2):
                for p in range(2):
                    part = done[4 * t + 2 * p : 4 * t + 2 * p + 2, :].astype(jnp.bfloat16)
                    coef_send[b, t, p, :, g * LANES : (g + 1) * LANES] = part
                    place = pl.ds(pl.multiple_of(lo * (cols // 4) + g * LANES, LANES), LANES)
                    coef_out[t, 2 * b + p, :, place] = part
        for d in range(1, n_lon):
            coef_copy(b, d).start()
        return 0

    lax.fori_loop(0, blocks, third, 0)

    def finish(b, _):
        for d in range(1, n_lon):
            coef_copy(b, d).wait()
        side_copy(b, 0).wait_send()
        side_copy(b, 1).wait_send()

        @pl.when(has_below)
        def _():
            row_copy(b, 0).wait_send()

        @pl.when(has_above)
        def _():
            row_copy(b, 1).wait_send()

        return 0

    lax.fori_loop(0, blocks, finish, 0)


def on_device(n_lat, n_lon, heat, salt, east, pole, spin, sea, depth):
    levels, rows, cols = heat.shape
    chunks, blocks = cols // LANES, levels // BLOCK
    tall = chunks * rows
    total = levels * tall
    field = pltpu.VMEM((total, LANES), jnp.float32)
    longer = pltpu.VMEM((total + tall, LANES), jnp.float32)
    dma = pltpu.SemaphoreType.DMA
    hbm = pl.BlockSpec(memory_space=pl.ANY)

    def tiled(x):
        x = x.reshape(x.shape[:-1] + (chunks, LANES))
        return jnp.swapaxes(x, -3, -2).reshape(-1, LANES)

    def whole(x):
        return jnp.swapaxes(x.reshape(levels, chunks, rows, LANES), 1, 2).reshape(levels, rows, cols)

    outs = pl.pallas_call(
        functools.partial(step_kernel, n_lat, n_lon),
        out_shape=[OUT_SPACE((total, LANES), jnp.float32)] * 4
        + [OUT_SPACE((2, 2 * blocks, 2, n_lon * cols // 4), jnp.bfloat16)],
        in_specs=[pl.BlockSpec(memory_space=pltpu.SMEM)] + [hbm] * 6,
        out_specs=[pl.BlockSpec(memory_space=pltpu.VMEM)] * 5,
        scratch_shapes=[
            longer,
            longer,
            field,
            field,
            pltpu.VMEM((total, LANES), jnp.int32),
            pltpu.VMEM((tall, LANES), jnp.int32),
            longer,
            field,
            pltpu.VMEM((2, blocks, 4 * BLOCK, cols), jnp.bfloat16),
            pltpu.VMEM((blocks, 4 * BLOCK, cols), jnp.bfloat16),
            pltpu.VMEM((blocks, 4 * BLOCK, cols), jnp.bfloat16),
            pltpu.VMEM((LANES, LANES), jnp.float32),
            pltpu.VMEM((blocks, ROWS, LANES), jnp.float32),
            pltpu.VMEM((blocks, ROWS, LANES), jnp.float32),
            pltpu.VMEM((blocks, ROWS, LANES), jnp.float32),
            pltpu.VMEM((LANES, LANES), jnp.float32),
            pltpu.VMEM((LANES, LANES), jnp.float32),
            pltpu.VMEM((2 * tall, LANES), jnp.float32),
            pltpu.VMEM((2 * tall, LANES), jnp.float32),
            pltpu.VMEM((4 * LANES, LANES), jnp.float32),
            pltpu.VMEM((ROWS, 4 * ROWS), jnp.float32),
            pltpu.VMEM((cols // (4 * LANES) * 4 * ROWS, 4 * LANES), jnp.float32),
            pltpu.VMEM((blocks, 2, 2, 2, cols // 4), jnp.bfloat16),
            dma((5, blocks)),
            dma,
            dma((2, blocks)),
            dma((blocks,)),
            dma((blocks,)),
            dma((2, blocks)),
            dma((blocks,)),
            dma((blocks,)),
            dma((blocks, n_lon)),
            dma((blocks, n_lon)),
        ],
        compiler_params=pltpu.CompilerParams(collective_id=0, has_side_effects=True, vmem_limit_bytes=28 << 20),
        name="ocean_step",
    )(
        spin, tiled(heat), tiled(salt), tiled(east), tiled(pole), tiled(sea), tiled(depth)
    )
    return tuple(whole(x) for x in outs[:4]) + (outs[4],)


OUT_SPACE = jax.ShapeDtypeStruct


def solution(mesh):
    field = P(None, "lat", "lon")
    return jax.shard_map(
        functools.partial(on_device, mesh.shape["lat"], mesh.shape["lon"]),
        mesh=mesh,
        in_specs=(field, field, field, field, P("lat"), field, P("lat", "lon")),
        out_specs=(field, field, field, field, P(None, None, "lat", None)),
        check_vma=False,
    )
```

```python
import functools
import math

import jax
import jax.numpy as jnp
from jax import lax
from jax.experimental import pallas as pl
from jax.experimental.pallas import tpu as pltpu
from jax.sharding import PartitionSpec as P

MESH = pl.DeviceIdType.MESH
BUOY_SALT = 0.25 * 0.25 * 0.8
BUOY_HEAT = 0.25 * 0.25 * 0.2
CARRY = 0.2 * 0.25
MIX = 0.2 * 0.8
VERT = 0.1
FLAT = math.sqrt(1.0 / 8.0)
WAVE = [math.sqrt(2.0 / 8.0) * math.cos(math.pi * (2 * n + 1) / 16.0) for n in range(8)]
ROWS = 8
LANES = 128
BLOCK = 8


def pairwise_sum(parts):
    while len(parts) > 1:
        parts = [sum(parts[i : i + 2][1:], parts[i]) for i in range(0, len(parts), 2)]
    return parts[0]


def table_value(freq, place):
    wave = jnp.full(freq.shape, WAVE[0], jnp.float32)
    for n in range(1, 8):
        wave = jnp.where(place == n, WAVE[n], wave)
    return jnp.where(freq == 0, FLAT, wave)


def fluxes(near, far, both, pairs):
    t = CARRY * (near + far)
    a = both * (t + MIX)
    b = both * (t - MIX)
    return [a * q + b * n for q, n in pairs]


REVERSED = (0, 4, 2, 6, 1, 5, 3, 7)


def edge_rows(x, row):
    y = [x[i] for i in REVERSED]
    ends = (row == 0) | (row == ROWS - 1)
    outer = ends | (row == 3) | (row == 4)
    even = lax.rem(row, 2) == 0
    pairs = [jnp.where(ends, y[i], pltpu.roll(y[i + 1], 4, 0)) for i in range(0, 8, 2)]
    low, high = (jnp.where(outer, pairs[i], pltpu.roll(pairs[i + 1], 2, 0)) for i in (0, 2))
    high = pltpu.roll(high, 1, 0)
    return jnp.where(even, low, high), pltpu.roll(jnp.where(even, high, low), 1, 0)


def step_kernel(
    n_lat,
    n_lon,
    spin_hbm,
    heat_hbm,
    salt_hbm,
    east_hbm,
    pole_hbm,
    sea_hbm,
    depth_hbm,
    heat_out,
    salt_out,
    east_out,
    pole_out,
    coef_out,
    heat,
    salt,
    east,
    pole,
    sea,
    depth,
    wet,
    press,
    row_send,
    from_south,
    from_north,
    edge_box,
    side_send,
    from_west,
    from_east,
    halo_box,
    halo_cols,
    upward,
    below_sum,
    tower,
    own_edge,
    edge_value,
    lane_table,
    stack,
    coef_send,
    spin,
    load_sem,
    depth_sem,
    spin_sem,
    row_send_sem,
    south_sem,
    north_sem,
    side_send_sem,
    west_sem,
    east_sem,
    coef_send_sem,
    coef_sem,
    partner_sem,
    coef_keep_sem,
):
    chunks = depth.shape[0] // ROWS
    cols = chunks * LANES
    tall = chunks * ROWS
    total = press.shape[0]
    blocks = total // (tall * BLOCK)
    slab = BLOCK * ROWS
    la = lax.axis_index("lat")
    lo = lax.axis_index("lon")
    above = {"lat": lax.rem(la + 1, n_lat)}
    below = {"lat": lax.rem(la + n_lat - 1, n_lat)}
    right = {"lon": lax.rem(lo + 1, n_lon)}
    left = {"lon": lax.rem(lo + n_lon - 1, n_lon)}
    has_above = la < n_lat - 1
    has_below = la > 0

    fields = ((heat_hbm, heat), (salt_hbm, salt), (sea_hbm, sea), (east_hbm, east), (pole_hbm, pole))

    def load(i, b):
        hbm, vmem = fields[i]
        part = pl.ds(pl.multiple_of(b * BLOCK * tall, BLOCK * tall), BLOCK * tall)
        return pltpu.make_async_copy(hbm.at[part], vmem.at[part], load_sem.at[b])

    barrier = pltpu.get_barrier_semaphore()
    peers = [above, below] + [{"lon": lax.rem(lo + d, n_lon)} for d in range(1, n_lon)]
    for peer in peers:
        pl.semaphore_signal(barrier, inc=1, device_id=peer, device_id_type=MESH)

    depth_load = pltpu.make_async_copy(depth_hbm, depth, depth_sem)
    depth_load.start()
    spin_load = pltpu.make_async_copy(spin_hbm, spin, spin_sem)
    spin_load.start()
    for b in range(blocks):
        for i in range(len(fields)):
            load(i, b).start()

    lane = lax.broadcasted_iota(jnp.int32, (ROWS, LANES), 1)
    row = lax.broadcasted_iota(jnp.int32, (ROWS, LANES), 0)
    zero = jnp.zeros((ROWS, LANES), jnp.float32)

    deep = lane_table.shape[0]
    n = lax.broadcasted_iota(jnp.int32, (deep, LANES), 0)
    o = lax.broadcasted_iota(jnp.int32, (deep, LANES), 1)
    table = jnp.where(n // 8 == o // 2, table_value(o % 2, n % 8), 0.0)
    high = table.astype(jnp.bfloat16)
    lane_table[:, :LANES] = high
    lane_table[:, LANES:] = (table - high.astype(jnp.float32)).astype(jnp.bfloat16)
    row_wave = table_value(jnp.ones_like(row), row)
    edge_box[...] = jnp.zeros_like(edge_box)
    halo_box[...] = jnp.zeros_like(halo_box)
    upward[...] = jnp.zeros_like(upward)
    below_sum[...] = jnp.zeros_like(below_sum)
    tower[...] = jnp.zeros_like(tower)
    for f in (heat, salt, wet):
        f[total:, :] = jnp.zeros((tall, LANES), jnp.float32)

    @pl.when(la == 0)
    def _():
        from_south[...] = jnp.zeros_like(from_south)

    @pl.when(la == n_lat - 1)
    def _():
        from_north[...] = jnp.zeros_like(from_north)

    spin_load.wait()
    spin_half = jnp.full((ROWS, LANES), 0.5 * spin[0], jnp.float32)
    for j in range(1, ROWS):
        spin_half = jnp.where(row == j, 0.5 * spin[j], spin_half)
    depth_load.wait()
    pl.semaphore_wait(barrier, len(peers))

    def at(k, c):
        return pl.ds(pl.multiple_of(k * tall, tall) + c * ROWS, ROWS)

    def tile(i):
        return pl.ds(pl.multiple_of(i * ROWS, ROWS), ROWS)

    def own(b, side, f, c):
        return tile(((b * 2 + side) * 5 + f) * chunks + c)

    def row_copy(b, side):
        return pltpu.make_async_remote_copy(
            src_ref=row_send.at[side, b],
            dst_ref=(from_north if side == 0 else from_south).at[b],
            send_sem=row_send_sem.at[side],
            recv_sem=(north_sem if side == 0 else south_sem).at[b],
            device_id=below if side == 0 else above,
            device_id_type=MESH,
        )

    def side_copy(b, side):
        return pltpu.make_async_remote_copy(
            src_ref=side_send.at[b],
            dst_ref=(from_east if side == 0 else from_west).at[b],
            send_sem=side_send_sem.at[side],
            recv_sem=(east_sem if side == 0 else west_sem).at[b],
            device_id=left if side == 0 else right,
            device_id_type=MESH,
        )

    partner = lo + 1 - 2 * lax.rem(lo, 2)
    width = cols // 4

    def place(owner):
        return pl.ds(pl.multiple_of(owner * width, LANES), width)

    def coef_copy(b, kind, dy=0):
        ahead_y = lax.rem(lo + 2 * dy, n_lon)
        target = (partner, ahead_y, ahead_y, lax.rem(partner + 2 * dy, n_lon))[kind]
        owner = partner if kind == 2 else lo
        there = coef_out.at[:, pl.ds(2 * b, 2), :, place(owner)]
        return pltpu.make_async_remote_copy(
            src_ref=there if kind == 2 else coef_send.at[b],
            dst_ref=there,
            send_sem=coef_send_sem,
            recv_sem=partner_sem.at[b] if kind == 0 else coef_sem,
            device_id={"lon": target},
            device_id_type=MESH,
        )

    def coef_keep(b):
        here = coef_out.at[:, pl.ds(2 * b, 2), :, place(lo)]
        return pltpu.make_async_copy(coef_send.at[b], here, coef_keep_sem)

    turns = range(1, n_lon // 2)

    def first(b, _):
        pltpu.make_async_copy(heat_hbm, heat.at[pl.ds(0, total)], load_sem.at[b]).wait()
        for c in range(chunks):
            deep = depth[c * ROWS : (c + 1) * ROWS, :]
            s = below_sum[c * ROWS : (c + 1) * ROWS, :]
            cells = []
            for i in range(BLOCK):
                k = b * BLOCK + i
                here = at(k, c)
                w = jnp.where(k < deep, sea[here, :], 0).astype(jnp.float32)
                t, q = heat[here, :], salt[here, :]
                d = w * (BUOY_SALT * q - BUOY_HEAT * t)
                s = s + d
                p = s - 0.5 * d
                wet[here, :] = w
                press[here, :] = p
                inner = jnp.where(row == 0, -pltpu.roll(p, ROWS - 1, 0), pltpu.roll(p, 1, 0))
                cells.append((t, q, w, w * ((pole[here, :] - spin_half * east[here, :]) + inner), p))
            below_sum[c * ROWS : (c + 1) * ROWS, :] = s
            edges = [edge_rows(x, row) for x in zip(*cells)]
            ch = slice(c * LANES, (c + 1) * LANES)
            for side in range(2):
                for f in range(5):
                    own_edge[own(b, side, f, c), :] = edges[f][side]
                for f in (0, 2):
                    pair = jnp.concatenate([edges[f][side], edges[f + 1][side]], 0)
                    row_send[side, b, 8 * f : 8 * f + 16, ch] = pair.astype(jnp.bfloat16)

        @pl.when(has_below)
        def _():
            row_copy(b, 0).start()

        @pl.when(has_above)
        def _():
            row_copy(b, 1).start()

        for i in range(BLOCK):
            for side in range(2):
                here = at(b * BLOCK + i, 0 if side == 0 else chunks - 1)
                p = press[here, :]
                w = wet[here, :]
                flow = east[here, :] + spin_half * pole[here, :]
                if side == 0:
                    part = w * (flow - pltpu.roll(p, LANES - 1, 1))
                else:
                    part = w * (flow + pltpu.roll(p, 1, 1))
                box = zero
                for f, v in enumerate((heat[here, :], salt[here, :], w, part, p)):
                    shift = f if side == 0 else f + 1
                    v = pltpu.roll(v, shift, 1) if shift else v
                    box = jnp.where(lane == f, v, box)
                edge_box[side * slab + i * ROWS : side * slab + (i + 1) * ROWS, :] = box
        side_send[b] = edge_box[...].T[:ROWS, :]
        side_copy(b, 0).start()
        side_copy(b, 1).start()
        return 0

    lax.fori_loop(0, blocks, first, 0)

    def second(b, _):
        side_copy(b, 0).wait_recv()
        side_copy(b, 1).wait_recv()
        halo_box[0:ROWS, :] = jnp.where(lane < slab, from_east[b], from_west[b])
        halo_cols[...] = halo_box[...].T

        for side in range(2):
            got = from_south if side == 0 else from_north

            @pl.when(has_below if side == 0 else has_above)
            def _():
                row_copy(b, 1 - side).wait_recv()

            for c in range(chunks):
                ch = slice(c * LANES, (c + 1) * LANES)
                q0, q1, w, part, p = (own_edge[own(b, side, f, c), :] for f in range(5))
                tracers = got[b, 0:16, ch].astype(jnp.float32)
                rest = got[b, 16:32, ch].astype(jnp.float32)
                far0, far1, w_far, v_far = tracers[0:8], tracers[8:16], rest[0:8], rest[8:16]
                d = w_far * (BUOY_SALT * far1 - BUOY_HEAT * far0)
                s = d
                for gap in (1, 2, 4):
                    s = s + jnp.where(row >= gap, pltpu.roll(s, gap, 0), 0.0)
                held = slice((side * chunks + c) * ROWS, (side * chunks + c + 1) * ROWS)
                s = s + tower[held, :]
                tower[held, :] = jnp.broadcast_to(s[BLOCK - 1 : BLOCK, :], (BLOCK, LANES))
                p_far = s - 0.5 * d
                if side == 0:
                    v = part + w * p_far
                    v_far = v_far - w_far * p
                    flux = fluxes(v_far, v, w * w_far, [(far0, q0), (far1, q1)])
                else:
                    v = part - w * p_far
                    v_far = v_far + w_far * p
                    flux = fluxes(v, v_far, w * w_far, [(q0, far0), (q1, far1)])
                for f, x in enumerate((v, *flux)):
                    edge_value[tile((side * 3 + f) * chunks + c), :] = x

        def level(i, _):
            k = b * BLOCK + i
            over_east = halo_cols[pl.ds(pl.multiple_of(i * ROWS, ROWS), ROWS), :]
            over_west = halo_cols[pl.ds(pl.multiple_of(slab + i * ROWS, ROWS), ROWS), :]
            last = LANES - 1

            def chunk(ref, c):
                return ref[at(k, c), :]

            def edge(side, f, c):
                line = pl.ds(((side * 3 + f) * chunks + c) * ROWS + i, 1)
                return jnp.broadcast_to(edge_value[line, :], (ROWS, LANES))

            def to_last(f):
                return pltpu.roll(over_east, last - f, 1)

            def to_first(f):
                return pltpu.roll(over_west, LANES - f, 1) if f else over_west

            def ahead(turned, c):
                return jnp.where(lane == last, turned[c + 1], turned[c])

            p = [chunk(press, c) for c in range(chunks)]
            w = [chunk(wet, c) for c in range(chunks)]
            p_ahead = [pltpu.roll(x, last, 1) for x in p] + [to_last(4)]
            p_back = [to_first(4)] + [pltpu.roll(x, 1, 1) for x in p]
            u, v = [], []
            for c in range(chunks):
                e, n = chunk(east, c), chunk(pole, c)
                dx = ahead(p_ahead, c) - jnp.where(lane == 0, p_back[c], p_back[c + 1])
                u.append(w[c] * (e + (spin_half * n - dx)))
                dy = pltpu.roll(p[c], ROWS - 1, 0) - pltpu.roll(p[c], 1, 0)
                inside = w[c] * (n - (spin_half * e + dy))
                v.append(jnp.where(row == 0, edge(0, 0, c), jnp.where(row == ROWS - 1, edge(1, 0, c), inside)))
                east_out[at(k, c), :] = u[c]
                pole_out[at(k, c), :] = v[c]

            q = [[chunk(f, c) for c in range(chunks)] for f in (heat, salt)]
            w_ahead = [pltpu.roll(x, last, 1) for x in w] + [to_last(2)]
            u_ahead = [pltpu.roll(x, last, 1) for x in u]
            u_ahead.append(to_last(3) + to_last(2) * p[chunks - 1])
            q_ahead = [
                [pltpu.roll(x, last, 1) for x in q[t]] + [to_last(t)] for t in range(2)
            ]
            w_out = to_first(2)
            u_out = to_first(3) - w_out * p[0]
            flux_back = fluxes(
                u_out, u[0], w_out * w[0], [(to_first(t), q[t][0]) for t in range(2)]
            )
            for c in range(chunks):
                flux = fluxes(
                    u[c],
                    ahead(u_ahead, c),
                    w[c] * ahead(w_ahead, c),
                    [(q[t][c], ahead(q_ahead[t], c)) for t in range(2)],
                )
                turned = [pltpu.roll(x, 1, 1) for x in flux]
                flux_n = fluxes(
                    v[c],
                    pltpu.roll(v[c], ROWS - 1, 0),
                    w[c] * pltpu.roll(w[c], ROWS - 1, 0),
                    [(q[t][c], pltpu.roll(q[t][c], ROWS - 1, 0)) for t in range(2)],
                )
                both = VERT * (w[c] * wet[at(k + 1, c), :])
                for t, (f, out) in enumerate(((heat, heat_out), (salt, salt_out))):
                    above_q = f[at(k + 1, c), :]
                    rise = both * (above_q - q[t][c])
                    held = slice((t * chunks + c) * ROWS, (t * chunks + c + 1) * ROWS)
                    gain = rise - upward[held, :]
                    upward[held, :] = rise
                    dx = flux[t] - jnp.where(lane == 0, flux_back[t], turned[t])
                    over = jnp.where(row == ROWS - 1, edge(1, t + 1, c), flux_n[t])
                    dy = over - jnp.where(row == 0, edge(0, t + 1, c), pltpu.roll(flux_n[t], 1, 0))
                    out[at(k, c), :] = w[c] * ((q[t][c] + gain) - (dx + dy))
                flux_back = turned
            return 0

        lax.fori_loop(0, BLOCK, level, 0)

        groups = chunks // 4
        half = groups * 4 * ROWS
        for c in range(chunks):
            g, across = c // 4, slice((c % 4) * LANES, (c % 4 + 1) * LANES)
            for t, f in enumerate((heat_out, salt_out)):
                x = [f[at(b * BLOCK + i, c), :] for i in range(BLOCK)]
                add = [x[i] + x[BLOCK - 1 - i] for i in range(BLOCK // 2)]
                dif = [WAVE[i] * (x[i] - x[BLOCK - 1 - i]) for i in range(BLOCK // 2)]
                both = jnp.concatenate([FLAT * pairwise_sum(add), pairwise_sum(dif)], 0)
                high = both.astype(jnp.bfloat16)
                base = (g * 2 + t) * 2 * ROWS
                stack[base : base + 2 * ROWS, across] = high
                stack[half + base : half + base + 2 * ROWS, across] = (both - high.astype(jnp.float32)).astype(jnp.bfloat16)
        wide = jnp.dot(stack[...], lane_table[...], preferred_element_type=jnp.float32)
        short = (wide[:half, :LANES] + wide[half:, :LANES]) + (wide[:half, LANES:] + wide[half:, LANES:])
        for g in range(groups):
            for t in range(2):
                for p in range(2):
                    base = ((g * 2 + t) * 2 + p) * ROWS
                    z = short[base : base + ROWS, :]
                    flat, wave = FLAT * z, row_wave * z
                    z = jnp.where(row < 4, flat + pltpu.roll(flat, 4, 0), wave + pltpu.roll(wave, 4, 0))
                    z = z + pltpu.roll(z, 2, 0)
                    z = z + pltpu.roll(z, 1, 0)
                    z = jnp.where(row == 0, pltpu.roll(z, 5, 0), pltpu.roll(z, 2, 0))
                    coef_send[b, t, p, :, g * LANES : (g + 1) * LANES] = z[0:2, :].astype(jnp.bfloat16)
        coef_copy(b, 0).start()
        for dy in turns:
            coef_copy(b, 1, dy).start()

        @pl.when(b == blocks - 1)
        def _():
            for dy in turns:
                coef_copy(b, 3, dy).start()

        coef_keep(b).start()

        @pl.when(b > 0)
        def _():
            coef_copy(b - 1, 0).wait_recv()
            for dy in turns:
                coef_copy(b - 1, 2, dy).start()

        return 0

    lax.fori_loop(0, blocks, second, 0)

    coef_copy(blocks - 1, 0).wait_recv()

    def settle(ref, sem):
        pltpu.make_async_copy(ref, ref, sem).wait()

    settle(coef_out.at[:, :, :, pl.ds(0, width * (n_lon - 2))], coef_sem)
    settle(coef_out.at[:, :, :, pl.ds(0, width * (n_lon - 1))], coef_send_sem)
    settle(coef_send, coef_keep_sem)
    settle(side_send, side_send_sem.at[0])
    settle(side_send, side_send_sem.at[1])

    @pl.when(has_below)
    def _():
        settle(row_send.at[0], row_send_sem.at[0])

    @pl.when(has_above)
    def _():
        settle(row_send.at[1], row_send_sem.at[1])


def deliver_kernel(pieces, *refs):
    count = len(refs) // 2
    sources, places, sem = refs[:count], refs[count : 2 * count], refs[-1]
    copies = []
    for i, (source, target) in enumerate(zip(sources, places)):
        parts = pieces if source.shape[0] % (8 * pieces) == 0 else 1
        size = source.shape[0] // parts
        for p in range(parts):
            part = pl.ds(p * size, size)
            copies.append(pltpu.make_async_copy(source.at[part], target.at[part], sem.at[i, p]))
    for copy in copies:
        copy.start()
    for copy in copies:
        copy.wait()


def deliver(arrays, pieces=4):
    return pl.pallas_call(
        functools.partial(deliver_kernel, pieces),
        out_shape=[pltpu.HBM(x.shape, x.dtype) for x in arrays],
        in_specs=[pl.BlockSpec(memory_space=pltpu.VMEM)] * len(arrays),
        out_specs=[pl.BlockSpec(memory_space=pl.ANY)] * len(arrays),
        scratch_shapes=[pltpu.SemaphoreType.DMA((len(arrays), pieces))],
        compiler_params=pltpu.CompilerParams(vmem_limit_bytes=1 << 20),
        name="deliver",
    )(*(pltpu.with_memory_space_constraint(x, pltpu.VMEM) for x in arrays))


def on_device(n_lat, n_lon, heat, salt, east, pole, spin, sea, depth):
    levels, rows, cols = heat.shape
    chunks, blocks = cols // LANES, levels // BLOCK
    tall = chunks * rows
    total = levels * tall
    field = pltpu.VMEM((total, LANES), jnp.float32)
    longer = pltpu.VMEM((total + tall, LANES), jnp.float32)
    dma = pltpu.SemaphoreType.DMA
    hbm = pl.BlockSpec(memory_space=pl.ANY)

    def tiled(x):
        x = x.reshape(x.shape[:-1] + (chunks, LANES))
        return jnp.swapaxes(x, -3, -2).reshape(-1, LANES)

    def whole(x):
        return jnp.swapaxes(x.reshape(levels, chunks, rows, LANES), 1, 2).reshape(levels, rows, cols)

    outs = pl.pallas_call(
        functools.partial(step_kernel, n_lat, n_lon),
        out_shape=[pltpu.VMEM((total, LANES), jnp.float32)] * 4
        + [pltpu.VMEM((2, 2 * blocks, 2, n_lon * cols // 4), jnp.bfloat16)],
        in_specs=[hbm] * 7,
        out_specs=[pl.BlockSpec(memory_space=pltpu.VMEM)] * 5,
        scratch_shapes=[
            longer,
            longer,
            field,
            field,
            pltpu.VMEM((total, LANES), jnp.int32),
            pltpu.VMEM((tall, LANES), jnp.int32),
            longer,
            field,
            pltpu.VMEM((2, blocks, 4 * BLOCK, cols), jnp.bfloat16),
            pltpu.VMEM((blocks, 4 * BLOCK, cols), jnp.bfloat16),
            pltpu.VMEM((blocks, 4 * BLOCK, cols), jnp.bfloat16),
            pltpu.VMEM((LANES, LANES), jnp.float32),
            pltpu.VMEM((blocks, ROWS, LANES), jnp.float32),
            pltpu.VMEM((blocks, ROWS, LANES), jnp.float32),
            pltpu.VMEM((blocks, ROWS, LANES), jnp.float32),
            pltpu.VMEM((LANES, LANES), jnp.float32),
            pltpu.VMEM((LANES, LANES), jnp.float32),
            pltpu.VMEM((2 * tall, LANES), jnp.float32),
            pltpu.VMEM((tall, LANES), jnp.float32),
            pltpu.VMEM((2 * tall, LANES), jnp.float32),
            pltpu.VMEM((blocks * 2 * 5 * tall, LANES), jnp.float32),
            pltpu.VMEM((2 * 3 * tall, LANES), jnp.float32),
            pltpu.VMEM((4 * LANES, 2 * LANES), jnp.bfloat16),
            pltpu.VMEM((chunks // 4 * 8 * ROWS, 4 * LANES), jnp.bfloat16),
            pltpu.VMEM((blocks, 2, 2, 2, cols // 4), jnp.bfloat16),
            pltpu.SMEM((rows,), jnp.float32),
            dma((blocks,)),
            dma,
            dma,
            dma((2,)),
            dma((blocks,)),
            dma((blocks,)),
            dma((2,)),
            dma((blocks,)),
            dma((blocks,)),
            dma,
            dma,
            dma((blocks,)),
            dma,
        ],
        compiler_params=pltpu.CompilerParams(collective_id=0, has_side_effects=True, vmem_limit_bytes=28 << 20),
        name="ocean_step",
    )(
        *(
            pltpu.with_memory_space_constraint(x, pltpu.HBM)
            for x in (spin, tiled(heat), tiled(salt), tiled(east), tiled(pole), tiled(sea), tiled(depth))
        )
    )
    outs = deliver(outs)
    return tuple(whole(x) for x in outs[:4]) + (outs[4],)


def solution(mesh):
    field = P(None, "lat", "lon")
    return jax.shard_map(
        functools.partial(on_device, mesh.shape["lat"], mesh.shape["lon"]),
        mesh=mesh,
        in_specs=(field, field, field, field, P("lat"), field, P("lat", "lon")),
        out_specs=(field, field, field, field, P(None, None, "lat", None)),
        check_vma=False,
    )
```

```python
import functools
import math

import jax
import jax.numpy as jnp
from jax import lax
from jax.experimental import pallas as pl
from jax.experimental.pallas import tpu as pltpu
from jax.sharding import PartitionSpec as P

MESH = pl.DeviceIdType.MESH
BUOY_SALT = 0.25 * 0.25 * 0.8
BUOY_HEAT = 0.25 * 0.25 * 0.2
CARRY = 0.2 * 0.25
MIX = 0.2 * 0.8
VERT = 0.1
FLAT = math.sqrt(1.0 / 8.0)
WAVE = [math.sqrt(2.0 / 8.0) * math.cos(math.pi * (2 * n + 1) / 16.0) for n in range(8)]
ROWS = 8
LANES = 128
BLOCK = 8


def once(make):
    made = {}

    def get(c):
        if c not in made:
            made[c] = make(c)
        return made[c]

    return get


def pairwise_sum(parts):
    while len(parts) > 1:
        parts = [sum(parts[i : i + 2][1:], parts[i]) for i in range(0, len(parts), 2)]
    return parts[0]


def table_value(freq, place):
    wave = jnp.full(freq.shape, WAVE[0], jnp.float32)
    for n in range(1, 8):
        wave = jnp.where(place == n, WAVE[n], wave)
    return jnp.where(freq == 0, FLAT, wave)


def fluxes(near, far, both, pairs):
    t = CARRY * (near + far)
    a = both * (t + MIX)
    b = both * (t - MIX)
    return [a * q + b * n for q, n in pairs]


REVERSED = (0, 4, 2, 6, 1, 5, 3, 7)


AT_ONCE = 2


def several(level, count):
    def turn(i, _):
        for j in range(count):
            level(i * count + j)
        return 0

    lax.fori_loop(0, BLOCK // count, turn, 0)


def edge_rows(x, row):
    y = [x[i] for i in REVERSED]
    ends = (row == 0) | (row == ROWS - 1)
    outer = ends | (row == 3) | (row == 4)
    even = lax.rem(row, 2) == 0
    pairs = [jnp.where(ends, y[i], pltpu.roll(y[i + 1], 4, 0)) for i in range(0, 8, 2)]
    low, high = (jnp.where(outer, pairs[i], pltpu.roll(pairs[i + 1], 2, 0)) for i in (0, 2))
    high = pltpu.roll(high, 1, 0)
    return jnp.where(even, low, high), pltpu.roll(jnp.where(even, high, low), 1, 0)


def step_kernel(
    n_lat,
    n_lon,
    spin_hbm,
    heat_hbm,
    salt_hbm,
    east_hbm,
    pole_hbm,
    sea_hbm,
    depth_hbm,
    heat_out,
    salt_out,
    east_out,
    pole_out,
    coef_out,
    heat,
    salt,
    east,
    pole,
    sea,
    depth,
    wet,
    press,
    row_send,
    from_south,
    from_north,
    edge_box,
    side_send,
    from_west,
    from_east,
    halo_box,
    halo_cols,
    upward,
    side_flux,
    below_sum,
    tower,
    own_edge,
    edge_value,
    lane_table,
    stack,
    coef_send,
    spin,
    load_sem,
    depth_sem,
    spin_sem,
    row_send_sem,
    south_sem,
    north_sem,
    side_send_sem,
    west_sem,
    east_sem,
    coef_send_sem,
    coef_sem,
    coef_keep_sem,
):
    chunks = depth.shape[0] // ROWS
    cols = chunks * LANES
    tall = chunks * ROWS
    total = press.shape[0]
    blocks = total // (tall * BLOCK)
    la = lax.axis_index("lat")
    lo = lax.axis_index("lon")
    above = {"lat": lax.rem(la + 1, n_lat)}
    below = {"lat": lax.rem(la + n_lat - 1, n_lat)}
    right = {"lon": lax.rem(lo + 1, n_lon)}
    left = {"lon": lax.rem(lo + n_lon - 1, n_lon)}
    has_above = la < n_lat - 1
    has_below = la > 0

    fields = ((heat_hbm, heat), (salt_hbm, salt), (sea_hbm, sea), (east_hbm, east), (pole_hbm, pole))

    def load(i, b):
        hbm, vmem = fields[i]
        part = pl.ds(pl.multiple_of(b * BLOCK * tall, BLOCK * tall), BLOCK * tall)
        return pltpu.make_async_copy(hbm.at[part], vmem.at[part], load_sem.at[b])

    barrier = pltpu.get_barrier_semaphore()
    peers = [above, below] + [{"lon": lax.rem(lo + d, n_lon)} for d in range(1, n_lon)]
    for peer in peers:
        pl.semaphore_signal(barrier, inc=1, device_id=peer, device_id_type=MESH)

    depth_load = pltpu.make_async_copy(depth_hbm, depth, depth_sem)
    depth_load.start()
    spin_load = pltpu.make_async_copy(spin_hbm, spin, spin_sem)
    spin_load.start()
    for b in range(blocks):
        for i in range(len(fields)):
            load(i, b).start()

    last = LANES - 1
    lane = lax.broadcasted_iota(jnp.int32, (ROWS, LANES), 1)
    row = lax.broadcasted_iota(jnp.int32, (ROWS, LANES), 0)
    zero = jnp.zeros((ROWS, LANES), jnp.float32)

    deep = lane_table.shape[0]
    n = lax.broadcasted_iota(jnp.int32, (deep, LANES), 0)
    o = lax.broadcasted_iota(jnp.int32, (deep, LANES), 1)
    table = jnp.where(n // 8 == o // 2, table_value(o % 2, n % 8), 0.0)
    high = table.astype(jnp.bfloat16)
    lane_table[:, :LANES] = high
    lane_table[:, LANES:] = (table - high.astype(jnp.float32)).astype(jnp.bfloat16)
    row_wave = table_value(jnp.ones_like(row), row)
    edge_box[...] = jnp.zeros_like(edge_box)
    halo_box[...] = jnp.zeros_like(halo_box)
    upward[...] = jnp.zeros_like(upward)
    below_sum[...] = jnp.zeros_like(below_sum)
    tower[...] = jnp.zeros_like(tower)
    for f in (heat, salt, wet):
        f[total:, :] = jnp.zeros((tall, LANES), jnp.float32)

    @pl.when(la == 0)
    def _():
        from_south[...] = jnp.zeros_like(from_south)

    @pl.when(la == n_lat - 1)
    def _():
        from_north[...] = jnp.zeros_like(from_north)

    spin_load.wait()
    spin_half = jnp.full((ROWS, LANES), 0.5 * spin[0], jnp.float32)
    for j in range(1, ROWS):
        spin_half = jnp.where(row == j, 0.5 * spin[j], spin_half)
    depth_load.wait()

    def at(k, c):
        return pl.ds(pl.multiple_of(k * tall, tall) + c * ROWS, ROWS)

    def tile(i):
        return pl.ds(pl.multiple_of(i * ROWS, ROWS), ROWS)

    def own(b, side, f, c):
        return tile(((b * 2 + side) * 5 + f) * chunks + c)

    def row_copy(b, side):
        return pltpu.make_async_remote_copy(
            src_ref=row_send.at[side, b],
            dst_ref=(from_north if side == 0 else from_south).at[b],
            send_sem=row_send_sem.at[side],
            recv_sem=(north_sem if side == 0 else south_sem).at[b],
            device_id=below if side == 0 else above,
            device_id_type=MESH,
        )

    def send_rows(b):
        @pl.when(has_below)
        def _():
            row_copy(b, 0).start()

        @pl.when(has_above)
        def _():
            row_copy(b, 1).start()

    def side_copy(b, side):
        return pltpu.make_async_remote_copy(
            src_ref=side_send.at[b],
            dst_ref=(from_east if side == 0 else from_west).at[b],
            send_sem=side_send_sem.at[side],
            recv_sem=(east_sem if side == 0 else west_sem).at[b],
            device_id=left if side == 0 else right,
            device_id_type=MESH,
        )

    width = cols // 4

    def place(owner):
        return pl.ds(pl.multiple_of(owner * width, LANES), width)

    def coef_copy(b, d):
        return pltpu.make_async_remote_copy(
            src_ref=coef_send.at[b],
            dst_ref=coef_out.at[:, pl.ds(2 * b, 2), :, place(lo)],
            send_sem=coef_send_sem,
            recv_sem=coef_sem,
            device_id={"lon": lax.rem(lo + d, n_lon)},
            device_id_type=MESH,
        )

    def coef_keep(b):
        here = coef_out.at[:, pl.ds(2 * b, 2), :, place(lo)]
        return pltpu.make_async_copy(coef_send.at[b], here, coef_keep_sem)

    def first(b, _):
        pltpu.make_async_copy(heat_hbm, heat.at[pl.ds(0, total)], load_sem.at[b]).wait()
        for c in range(chunks):
            deep = depth[c * ROWS : (c + 1) * ROWS, :]
            s = below_sum[c * ROWS : (c + 1) * ROWS, :]
            cells = []
            for i in range(BLOCK):
                k = b * BLOCK + i
                here = at(k, c)
                w = jnp.where(k < deep, sea[here, :], 0).astype(jnp.float32)
                t, q = heat[here, :], salt[here, :]
                d = w * (BUOY_SALT * q - BUOY_HEAT * t)
                s = s + d
                p = s - 0.5 * d
                wet[here, :] = w
                press[here, :] = p
                inner = jnp.where(row == 0, -pltpu.roll(p, ROWS - 1, 0), pltpu.roll(p, 1, 0))
                cells.append((t, q, w, w * ((pole[here, :] - spin_half * east[here, :]) + inner), p))
            below_sum[c * ROWS : (c + 1) * ROWS, :] = s
            edges = [edge_rows(x, row) for x in zip(*cells)]
            ch = slice(c * LANES, (c + 1) * LANES)
            for side in range(2):
                for f in range(5):
                    own_edge[own(b, side, f, c), :] = edges[f][side]
                for f in (0, 2):
                    pair = jnp.concatenate([edges[f][side], edges[f + 1][side]], 0)
                    row_send[side, b, 8 * f : 8 * f + 16, ch] = pair.astype(jnp.bfloat16)

        for i in range(BLOCK):
            k = b * BLOCK + i

            def ends(get):
                return jnp.where(lane == 0, get(at(k, 0)), get(at(k, chunks - 1)))

            p = [press[at(k, c), :] for c in (0, chunks - 1)]
            slope = jnp.where(lane == 0, -pltpu.roll(p[0], last, 1), pltpu.roll(p[1], 1, 1))
            w = ends(lambda x: wet[x, :])
            part = w * (ends(lambda x: east[x, :] + spin_half * pole[x, :]) + slope)
            box = zero
            values = (ends(lambda x: heat[x, :]), ends(lambda x: salt[x, :]), w, part, jnp.where(lane == 0, *p))
            for f, v in enumerate(values):
                box = jnp.where((lane == 2 * f) | (lane == 2 * f + 1), pltpu.roll(v, 2 * f + 1, 1), box)
            edge_box[i * ROWS : (i + 1) * ROWS, :] = box
        side_send[b] = edge_box[...].T[: 2 * ROWS, :]
        @pl.when(b == 0)
        def _():
            pl.semaphore_wait(barrier, len(peers))

        side_copy(b, 0).start()
        side_copy(b, 1).start()

        @pl.when(b == 0)
        def _():
            send_rows(0)

        @pl.when(b == blocks - 2)
        def _():
            send_rows(1)

        return 0

    lax.fori_loop(0, blocks, first, 0)
    for b in range(2, blocks):
        send_rows(b)

    def second(b, _):
        side_copy(b, 0).wait_recv()
        side_copy(b, 1).wait_recv()
        odd = lax.rem(lax.broadcasted_iota(jnp.int32, (2 * ROWS, LANES), 0), 2) == 1
        halo_box[0 : 2 * ROWS, :] = jnp.where(odd, from_east[b], from_west[b])
        halo_cols[...] = halo_box[...].T

        def halo(i):
            beyond = halo_cols[tile(i), :]

            def to_last(f):
                return pltpu.roll(beyond, last - (2 * f + 1), 1)

            def to_first(f):
                return pltpu.roll(beyond, LANES - 2 * f, 1) if f else beyond

            return to_last, to_first

        def ahead(turned, c):
            return jnp.where(lane == last, turned[c + 1], turned[c])

        def flow(i):
            k = b * BLOCK + i
            to_last, to_first = halo(i)
            p = [press[at(k, c), :] for c in range(chunks)]
            p_turn = [pltpu.roll(x, last, 1) for x in p] + [to_last(4)]
            p_back = [to_first(4)] + [pltpu.roll(x, 1, 1) for x in p]
            for c in range(chunks):
                here = at(k, c)
                dx = ahead(p_turn, c) - jnp.where(lane == 0, p_back[c], p_back[c + 1])
                east_out[here, :] = wet[here, :] * (east[here, :] + (spin_half * pole[here, :] - dx))

        def flux(i):
            k = b * BLOCK + i
            to_last, to_first = halo(i)
            u, w, t, q = ([f[at(k, c), :] for c in range(chunks)] for f in (east_out, wet, heat, salt))
            u_beyond = to_last(3) + to_last(2) * press[at(k, chunks - 1), :]
            u_turn, w_turn, t_turn, q_turn = (
                [pltpu.roll(x, last, 1) for x in f] + [beyond]
                for f, beyond in ((u, u_beyond), (w, to_last(2)), (t, to_last(0)), (q, to_last(1)))
            )
            w_out = to_first(2)
            u_out = to_first(3) - w_out * press[at(k, 0), :]
            out = fluxes(u_out, u[0], w_out * w[0], [(to_first(0), t[0]), (to_first(1), q[0])])
            for f in range(2):
                side_flux[spot(i, f, -1), :] = out[f]
            for c in range(chunks):
                out = fluxes(
                    u[c], ahead(u_turn, c), w[c] * ahead(w_turn, c), [(t[c], ahead(t_turn, c)), (q[c], ahead(q_turn, c))]
                )
                for f in range(2):
                    side_flux[spot(i, f, c), :] = out[f]

        def spot(i, f, c):
            return tile((i * 2 + f) * (chunks + 1) + c + 1)

        def gather(i):
            k = b * BLOCK + i
            x = [[side_flux[spot(i, f, c), :] for c in range(-1, chunks)] for f in range(2)]
            back = [[y[0]] + [pltpu.roll(z, 1, 1) for z in y[1:]] for y in x]
            for c in range(chunks):
                both = VERT * (wet[at(k, c), :] * wet[at(k + 1, c), :])
                for f, (field, out) in enumerate(((heat, heat_out), (salt, salt_out))):
                    q = field[at(k, c), :]
                    rise = both * (field[at(k + 1, c), :] - q)
                    held = slice((f * chunks + c) * ROWS, (f * chunks + c + 1) * ROWS)
                    gain = rise - upward[held, :]
                    upward[held, :] = rise
                    dx = x[f][c + 1] - jnp.where(lane == 0, back[f][c], back[f][c + 1])
                    out[at(k, c), :] = (q + gain) - dx

        for i in range(BLOCK + 2):
            if i < BLOCK:
                flow(i)
            if 0 < i <= BLOCK:
                flux(i - 1)
            if i > 1:
                gather(i - 2)
        return 0

    lax.fori_loop(0, blocks, second, 0)

    def third(b, _):
        for side in range(2):
            got = from_south if side == 0 else from_north

            @pl.when(has_below if side == 0 else has_above)
            def _():
                row_copy(b, 1 - side).wait_recv()

            for c in range(chunks):
                ch = slice(c * LANES, (c + 1) * LANES)
                q0, q1, w, part, p = (own_edge[own(b, side, f, c), :] for f in range(5))
                tracers = got[b, 0:16, ch].astype(jnp.float32)
                rest = got[b, 16:32, ch].astype(jnp.float32)
                far0, far1, w_far, v_far = tracers[0:8], tracers[8:16], rest[0:8], rest[8:16]
                d = w_far * (BUOY_SALT * far1 - BUOY_HEAT * far0)
                s = d
                for gap in (1, 2, 4):
                    s = s + jnp.where(row >= gap, pltpu.roll(s, gap, 0), 0.0)
                held = slice((side * chunks + c) * ROWS, (side * chunks + c + 1) * ROWS)
                s = s + tower[held, :]
                tower[held, :] = jnp.broadcast_to(s[BLOCK - 1 : BLOCK, :], (BLOCK, LANES))
                p_far = s - 0.5 * d
                if side == 0:
                    v = part + w * p_far
                    v_far = v_far - w_far * p
                    flux = fluxes(v_far, v, w * w_far, [(far0, q0), (far1, q1)])
                else:
                    v = part - w * p_far
                    v_far = v_far + w_far * p
                    flux = fluxes(v, v_far, w * w_far, [(q0, far0), (q1, far1)])
                for f, x in enumerate((v, *flux)):
                    edge_value[tile((side * 3 + f) * chunks + c), :] = x

        def level(i):
            k = b * BLOCK + i

            def edge(side, f, c):
                line = pl.ds(((side * 3 + f) * chunks + c) * ROWS + i, 1)
                return jnp.broadcast_to(edge_value[line, :], (ROWS, LANES))

            for c in range(chunks):
                here = at(k, c)
                p, w = press[here, :], wet[here, :]
                dy = pltpu.roll(p, ROWS - 1, 0) - pltpu.roll(p, 1, 0)
                v = w * (pole[here, :] - (spin_half * east[here, :] + dy))
                v = jnp.where(row == 0, edge(0, 0, c), jnp.where(row == ROWS - 1, edge(1, 0, c), v))
                pole_out[here, :] = v
                q = [heat[here, :], salt[here, :]]
                flux = fluxes(
                    v,
                    pltpu.roll(v, ROWS - 1, 0),
                    w * pltpu.roll(w, ROWS - 1, 0),
                    [(x, pltpu.roll(x, ROWS - 1, 0)) for x in q],
                )
                for f, out in enumerate((heat_out, salt_out)):
                    over = jnp.where(row == ROWS - 1, edge(1, f + 1, c), flux[f])
                    under = jnp.where(row == 0, edge(0, f + 1, c), pltpu.roll(flux[f], 1, 0))
                    out[here, :] = w * (out[here, :] - (over - under))

        several(level, AT_ONCE)

        groups = chunks // 4
        half = groups * 4 * ROWS
        for c in range(chunks):
            g, across = c // 4, slice((c % 4) * LANES, (c % 4 + 1) * LANES)
            for t, f in enumerate((heat_out, salt_out)):
                x = [f[at(b * BLOCK + i, c), :] for i in range(BLOCK)]
                add = [x[i] + x[BLOCK - 1 - i] for i in range(BLOCK // 2)]
                dif = [WAVE[i] * (x[i] - x[BLOCK - 1 - i]) for i in range(BLOCK // 2)]
                both = jnp.concatenate([FLAT * pairwise_sum(add), pairwise_sum(dif)], 0)
                high = both.astype(jnp.bfloat16)
                base = (g * 2 + t) * 2 * ROWS
                stack[base : base + 2 * ROWS, across] = high
                stack[half + base : half + base + 2 * ROWS, across] = (both - high.astype(jnp.float32)).astype(jnp.bfloat16)
        wide = jnp.dot(stack[...], lane_table[...], preferred_element_type=jnp.float32)
        short = (wide[:half, :LANES] + wide[half:, :LANES]) + (wide[:half, LANES:] + wide[half:, LANES:])
        for g in range(groups):
            for t in range(2):
                for p in range(2):
                    base = ((g * 2 + t) * 2 + p) * ROWS
                    z = short[base : base + ROWS, :]
                    flat, wave = FLAT * z, row_wave * z
                    z = jnp.where(row < 4, flat + pltpu.roll(flat, 4, 0), wave + pltpu.roll(wave, 4, 0))
                    z = z + pltpu.roll(z, 2, 0)
                    z = z + pltpu.roll(z, 1, 0)
                    z = jnp.where(row == 0, pltpu.roll(z, 5, 0), pltpu.roll(z, 2, 0))
                    coef_send[b, t, p, :, g * LANES : (g + 1) * LANES] = z[0:2, :].astype(jnp.bfloat16)
        for d in sorted(range(1, n_lon), key=lambda d: -min(d, n_lon - d)):
            coef_copy(b, d).start()
        coef_keep(b).start()
        return 0

    lax.fori_loop(0, blocks, third, 0)

    def settle(ref, sem):
        pltpu.make_async_copy(ref, ref, sem).wait()

    settle(coef_out.at[:, :, :, pl.ds(0, width * (n_lon - 1))], coef_sem)
    settle(coef_out.at[:, :, :, pl.ds(0, width * (n_lon - 1))], coef_send_sem)
    settle(coef_send, coef_keep_sem)
    settle(side_send, side_send_sem.at[0])
    settle(side_send, side_send_sem.at[1])

    @pl.when(has_below)
    def _():
        settle(row_send.at[0], row_send_sem.at[0])

    @pl.when(has_above)
    def _():
        settle(row_send.at[1], row_send_sem.at[1])


def deliver_kernel(pieces, *refs):
    count = len(refs) // 2
    sources, places, sem = refs[:count], refs[count : 2 * count], refs[-1]
    copies = []
    for i, (source, target) in enumerate(zip(sources, places)):
        parts = pieces if source.shape[0] % (8 * pieces) == 0 else 1
        size = source.shape[0] // parts
        for p in range(parts):
            part = pl.ds(p * size, size)
            copies.append(pltpu.make_async_copy(source.at[part], target.at[part], sem.at[i, p]))
    for copy in copies:
        copy.start()
    for copy in copies:
        copy.wait()


def deliver(arrays, pieces=4):
    return pl.pallas_call(
        functools.partial(deliver_kernel, pieces),
        out_shape=[pltpu.HBM(x.shape, x.dtype) for x in arrays],
        in_specs=[pl.BlockSpec(memory_space=pltpu.VMEM)] * len(arrays),
        out_specs=[pl.BlockSpec(memory_space=pl.ANY)] * len(arrays),
        scratch_shapes=[pltpu.SemaphoreType.DMA((len(arrays), pieces))],
        compiler_params=pltpu.CompilerParams(vmem_limit_bytes=1 << 20),
        name="deliver",
    )(*(pltpu.with_memory_space_constraint(x, pltpu.VMEM) for x in arrays))


def on_device(n_lat, n_lon, heat, salt, east, pole, spin, sea, depth):
    levels, rows, cols = heat.shape
    chunks, blocks = cols // LANES, levels // BLOCK
    tall = chunks * rows
    total = levels * tall
    field = pltpu.VMEM((total, LANES), jnp.float32)
    longer = pltpu.VMEM((total + tall, LANES), jnp.float32)
    dma = pltpu.SemaphoreType.DMA
    hbm = pl.BlockSpec(memory_space=pl.ANY)

    def tiled(x):
        x = x.reshape(x.shape[:-1] + (chunks, LANES))
        return jnp.swapaxes(x, -3, -2).reshape(-1, LANES)

    def whole(x):
        return jnp.swapaxes(x.reshape(levels, chunks, rows, LANES), 1, 2).reshape(levels, rows, cols)

    outs = pl.pallas_call(
        functools.partial(step_kernel, n_lat, n_lon),
        out_shape=[pltpu.VMEM((total, LANES), jnp.float32)] * 4
        + [pltpu.VMEM((2, 2 * blocks, 2, n_lon * cols // 4), jnp.bfloat16)],
        in_specs=[hbm] * 7,
        out_specs=[pl.BlockSpec(memory_space=pltpu.VMEM)] * 5,
        scratch_shapes=[
            longer,
            longer,
            field,
            field,
            pltpu.VMEM((total, LANES), jnp.int32),
            pltpu.VMEM((tall, LANES), jnp.int32),
            longer,
            field,
            pltpu.VMEM((2, blocks, 4 * BLOCK, cols), jnp.bfloat16),
            pltpu.VMEM((blocks, 4 * BLOCK, cols), jnp.bfloat16),
            pltpu.VMEM((blocks, 4 * BLOCK, cols), jnp.bfloat16),
            pltpu.VMEM((LANES, LANES), jnp.float32),
            pltpu.VMEM((blocks, 2 * ROWS, LANES), jnp.float32),
            pltpu.VMEM((blocks, 2 * ROWS, LANES), jnp.float32),
            pltpu.VMEM((blocks, 2 * ROWS, LANES), jnp.float32),
            pltpu.VMEM((LANES, LANES), jnp.float32),
            pltpu.VMEM((LANES, LANES), jnp.float32),
            pltpu.VMEM((2 * tall, LANES), jnp.float32),
            pltpu.VMEM((BLOCK * 2 * (chunks + 1) * ROWS, LANES), jnp.float32),
            pltpu.VMEM((tall, LANES), jnp.float32),
            pltpu.VMEM((2 * tall, LANES), jnp.float32),
            pltpu.VMEM((blocks * 2 * 5 * tall, LANES), jnp.float32),
            pltpu.VMEM((2 * 3 * tall, LANES), jnp.float32),
            pltpu.VMEM((4 * LANES, 2 * LANES), jnp.bfloat16),
            pltpu.VMEM((chunks // 4 * 8 * ROWS, 4 * LANES), jnp.bfloat16),
            pltpu.VMEM((blocks, 2, 2, 2, cols // 4), jnp.bfloat16),
            pltpu.SMEM((rows,), jnp.float32),
            dma((blocks,)),
            dma,
            dma,
            dma((2,)),
            dma((blocks,)),
            dma((blocks,)),
            dma((2,)),
            dma((blocks,)),
            dma((blocks,)),
            dma,
            dma,
            dma,
        ],
        compiler_params=pltpu.CompilerParams(collective_id=0, has_side_effects=True, vmem_limit_bytes=28 << 20),
        name="ocean_step",
    )(
        *(
            pltpu.with_memory_space_constraint(x, pltpu.HBM)
            for x in (spin, tiled(heat), tiled(salt), tiled(east), tiled(pole), tiled(sea), tiled(depth))
        )
    )
    outs = deliver(outs)
    return tuple(whole(x) for x in outs[:4]) + (outs[4],)


def solution(mesh):
    field = P(None, "lat", "lon")
    return jax.shard_map(
        functools.partial(on_device, mesh.shape["lat"], mesh.shape["lon"]),
        mesh=mesh,
        in_specs=(field, field, field, field, P("lat"), field, P("lat", "lon")),
        out_specs=(field, field, field, field, P(None, None, "lat", None)),
        check_vma=False,
    )
```

```python
import functools
import math

import jax
import jax.numpy as jnp
from jax import lax
from jax.experimental import pallas as pl
from jax.experimental.pallas import tpu as pltpu
from jax.sharding import PartitionSpec as P

MESH = pl.DeviceIdType.MESH
BUOY_SALT = 0.25 * 0.25 * 0.8
BUOY_HEAT = 0.25 * 0.25 * 0.2
CARRY = 0.2 * 0.25
MIX = 0.2 * 0.8
VERT = 0.1
FLAT = math.sqrt(1.0 / 8.0)
WAVE = [math.sqrt(2.0 / 8.0) * math.cos(math.pi * (2 * n + 1) / 16.0) for n in range(8)]
ROWS = 8
LANES = 128
BLOCK = 8


def once(make):
    made = {}

    def get(c):
        if c not in made:
            made[c] = make(c)
        return made[c]

    return get


def pairwise_sum(parts):
    while len(parts) > 1:
        parts = [sum(parts[i : i + 2][1:], parts[i]) for i in range(0, len(parts), 2)]
    return parts[0]


def table_value(freq, place):
    wave = jnp.full(freq.shape, WAVE[0], jnp.float32)
    for n in range(1, 8):
        wave = jnp.where(place == n, WAVE[n], wave)
    return jnp.where(freq == 0, FLAT, wave)


def fluxes(near, far, both, pairs):
    t = CARRY * (near + far)
    a = both * (t + MIX)
    b = both * (t - MIX)
    return [a * q + b * n for q, n in pairs]


REVERSED = (0, 4, 2, 6, 1, 5, 3, 7)


AT_ONCE = 2


def several(level, count):
    def turn(i, _):
        for j in range(count):
            level(i * count + j)
        return 0

    lax.fori_loop(0, BLOCK // count, turn, 0)


def edge_rows(x, row):
    y = [x[i] for i in REVERSED]
    ends = (row == 0) | (row == ROWS - 1)
    outer = ends | (row == 3) | (row == 4)
    even = lax.rem(row, 2) == 0
    pairs = [jnp.where(ends, y[i], pltpu.roll(y[i + 1], 4, 0)) for i in range(0, 8, 2)]
    low, high = (jnp.where(outer, pairs[i], pltpu.roll(pairs[i + 1], 2, 0)) for i in (0, 2))
    high = pltpu.roll(high, 1, 0)
    return jnp.where(even, low, high), pltpu.roll(jnp.where(even, high, low), 1, 0)


def step_kernel(
    n_lat,
    n_lon,
    spin_hbm,
    heat_hbm,
    salt_hbm,
    east_hbm,
    pole_hbm,
    sea_hbm,
    depth_hbm,
    heat_out,
    salt_out,
    east_out,
    pole_out,
    coef_out,
    heat,
    salt,
    east,
    pole,
    sea,
    depth,
    wet,
    press,
    row_send,
    from_south,
    from_north,
    edge_box,
    turned_box,
    side_send,
    from_west,
    from_east,
    halo_box,
    halo_cols,
    upward,
    side_flux,
    below_sum,
    tower,
    own_edge,
    edge_value,
    lane_table,
    stack,
    coef_send,
    spin,
    load_sem,
    depth_sem,
    spin_sem,
    row_send_sem,
    south_sem,
    north_sem,
    side_send_sem,
    west_sem,
    east_sem,
    coef_send_sem,
    coef_sem,
    coef_keep_sem,
):
    chunks = depth.shape[0] // ROWS
    cols = chunks * LANES
    tall = chunks * ROWS
    total = press.shape[0]
    blocks = total // (tall * BLOCK)
    la = lax.axis_index("lat")
    lo = lax.axis_index("lon")
    above = {"lat": lax.rem(la + 1, n_lat)}
    below = {"lat": lax.rem(la + n_lat - 1, n_lat)}
    right = {"lon": lax.rem(lo + 1, n_lon)}
    left = {"lon": lax.rem(lo + n_lon - 1, n_lon)}
    has_above = la < n_lat - 1
    has_below = la > 0

    fields = ((heat_hbm, heat), (salt_hbm, salt), (sea_hbm, sea), (east_hbm, east), (pole_hbm, pole))

    def load(i, b):
        hbm, vmem = fields[i]
        part = pl.ds(pl.multiple_of(b * BLOCK * tall, BLOCK * tall), BLOCK * tall)
        return pltpu.make_async_copy(hbm.at[part], vmem.at[part], load_sem.at[b])

    barrier = pltpu.get_barrier_semaphore()
    peers = [above, below] + [{"lon": lax.rem(lo + d, n_lon)} for d in range(1, n_lon)]
    for peer in peers:
        pl.semaphore_signal(barrier, inc=1, device_id=peer, device_id_type=MESH)

    depth_load = pltpu.make_async_copy(depth_hbm, depth, depth_sem)
    depth_load.start()
    spin_load = pltpu.make_async_copy(spin_hbm, spin, spin_sem)
    spin_load.start()
    for b in range(blocks):
        for i in range(len(fields)):
            load(i, b).start()

    last = LANES - 1
    lane = lax.broadcasted_iota(jnp.int32, (ROWS, LANES), 1)
    row = lax.broadcasted_iota(jnp.int32, (ROWS, LANES), 0)
    zero = jnp.zeros((ROWS, LANES), jnp.float32)

    deep = lane_table.shape[0]
    n = lax.broadcasted_iota(jnp.int32, (deep, LANES), 0)
    o = lax.broadcasted_iota(jnp.int32, (deep, LANES), 1)
    table = jnp.where(n // 8 == o // 2, table_value(o % 2, n % 8), 0.0)
    high = table.astype(jnp.bfloat16)
    lane_table[:, :LANES] = high
    lane_table[:, LANES:] = (table - high.astype(jnp.float32)).astype(jnp.bfloat16)
    row_wave = table_value(jnp.ones_like(row), row)
    edge_box[...] = jnp.zeros_like(edge_box)
    halo_box[...] = jnp.zeros_like(halo_box)
    upward[...] = jnp.zeros_like(upward)
    below_sum[...] = jnp.zeros_like(below_sum)
    tower[...] = jnp.zeros_like(tower)
    for f in (heat, salt, wet):
        f[total:, :] = jnp.zeros((tall, LANES), jnp.float32)

    @pl.when(la == 0)
    def _():
        from_south[...] = jnp.zeros_like(from_south)

    @pl.when(la == n_lat - 1)
    def _():
        from_north[...] = jnp.zeros_like(from_north)

    spin_load.wait()
    spin_half = jnp.full((ROWS, LANES), 0.5 * spin[0], jnp.float32)
    for j in range(1, ROWS):
        spin_half = jnp.where(row == j, 0.5 * spin[j], spin_half)
    depth_load.wait()

    def at(k, c):
        return pl.ds(pl.multiple_of(k * tall, tall) + c * ROWS, ROWS)

    def tile(i):
        return pl.ds(pl.multiple_of(i * ROWS, ROWS), ROWS)

    def own(b, side, f, c):
        return tile(((b * 2 + side) * 5 + f) * chunks + c)

    def row_copy(b, side):
        return pltpu.make_async_remote_copy(
            src_ref=row_send.at[side, b],
            dst_ref=(from_north if side == 0 else from_south).at[b],
            send_sem=row_send_sem.at[side],
            recv_sem=(north_sem if side == 0 else south_sem).at[b],
            device_id=below if side == 0 else above,
            device_id_type=MESH,
        )

    def send_rows(b):
        @pl.when(has_below)
        def _():
            row_copy(b, 0).start()

        @pl.when(has_above)
        def _():
            row_copy(b, 1).start()

    def side_copy(b, side):
        return pltpu.make_async_remote_copy(
            src_ref=side_send.at[side, b],
            dst_ref=(from_east if side == 0 else from_west).at[b],
            send_sem=side_send_sem.at[side],
            recv_sem=(east_sem if side == 0 else west_sem).at[b],
            device_id=left if side == 0 else right,
            device_id_type=MESH,
        )

    width = cols // 4

    def place(owner):
        return pl.ds(pl.multiple_of(owner * width, LANES), width)

    def coef_copy(b, d):
        return pltpu.make_async_remote_copy(
            src_ref=coef_send.at[b],
            dst_ref=coef_out.at[:, pl.ds(2 * b, 2), :, place(lo)],
            send_sem=coef_send_sem,
            recv_sem=coef_sem,
            device_id={"lon": lax.rem(lo + d, n_lon)},
            device_id_type=MESH,
        )

    def coef_keep(b):
        here = coef_out.at[:, pl.ds(2 * b, 2), :, place(lo)]
        return pltpu.make_async_copy(coef_send.at[b], here, coef_keep_sem)

    def first(b, _):
        pltpu.make_async_copy(heat_hbm, heat.at[pl.ds(0, total)], load_sem.at[b]).wait()
        for c in range(chunks):
            deep = depth[c * ROWS : (c + 1) * ROWS, :]
            s = below_sum[c * ROWS : (c + 1) * ROWS, :]
            cells = []
            for i in range(BLOCK):
                k = b * BLOCK + i
                here = at(k, c)
                w = jnp.where(k < deep, sea[here, :], 0).astype(jnp.float32)
                t, q = heat[here, :], salt[here, :]
                d = w * (BUOY_SALT * q - BUOY_HEAT * t)
                s = s + d
                p = s - 0.5 * d
                wet[here, :] = w
                press[here, :] = p
                inner = jnp.where(row == 0, -pltpu.roll(p, ROWS - 1, 0), pltpu.roll(p, 1, 0))
                cells.append((t, q, w, w * ((pole[here, :] - spin_half * east[here, :]) + inner), p))
            below_sum[c * ROWS : (c + 1) * ROWS, :] = s
            edges = [edge_rows(x, row) for x in zip(*cells)]
            ch = slice(c * LANES, (c + 1) * LANES)
            for side in range(2):
                for f in range(5):
                    own_edge[own(b, side, f, c), :] = edges[f][side]
                for f in (0, 2):
                    pair = jnp.concatenate([edges[f][side], edges[f + 1][side]], 0)
                    row_send[side, b, 8 * f : 8 * f + 16, ch] = pair.astype(jnp.bfloat16)

        for i in range(BLOCK):
            k = b * BLOCK + i

            def ends(get):
                return jnp.where(lane == 0, get(at(k, 0)), get(at(k, chunks - 1)))

            p = [press[at(k, c), :] for c in (0, chunks - 1)]
            slope = jnp.where(lane == 0, -pltpu.roll(p[0], last, 1), pltpu.roll(p[1], 1, 1))
            w = ends(lambda x: wet[x, :])
            part = w * (ends(lambda x: east[x, :] + spin_half * pole[x, :]) + slope)
            box = zero
            values = (ends(lambda x: heat[x, :]), ends(lambda x: salt[x, :]), w, part, jnp.where(lane == 0, *p))
            for f, v in enumerate(values):
                box = jnp.where((lane == 2 * f) | (lane == 2 * f + 1), pltpu.roll(v, 2 * f + 1, 1), box)
            edge_box[i * ROWS : (i + 1) * ROWS, :] = box
        turned_box[...] = edge_box[...].T[: 2 * ROWS, :]
        for side in range(2):
            side_send[side, b] = turned_box[pl.ds(1 - side, ROWS, stride=2), :]
        @pl.when(b == 0)
        def _():
            pl.semaphore_wait(barrier, len(peers))

        side_copy(b, 0).start()
        side_copy(b, 1).start()

        @pl.when(b == 0)
        def _():
            send_rows(0)

        @pl.when(b == blocks - 2)
        def _():
            send_rows(1)

        return 0

    lax.fori_loop(0, blocks, first, 0)
    for b in range(2, blocks):
        send_rows(b)

    def second(b, _):
        side_copy(b, 0).wait_recv()
        side_copy(b, 1).wait_recv()
        halo_box[0:ROWS, :] = from_east[b]
        halo_box[ROWS : 2 * ROWS, :] = from_west[b]
        halo_cols[...] = halo_box[...].T

        def halo(i):
            beyond = halo_cols[tile(i), :]

            def to_last(f):
                return pltpu.roll(beyond, last - f, 1)

            def to_first(f):
                return pltpu.roll(beyond, LANES - ROWS - f, 1)

            return to_last, to_first

        def ahead(turned, c):
            return jnp.where(lane == last, turned[c + 1], turned[c])

        def flow(i):
            k = b * BLOCK + i
            to_last, to_first = halo(i)
            p = [press[at(k, c), :] for c in range(chunks)]
            p_turn = [pltpu.roll(x, last, 1) for x in p] + [to_last(4)]
            p_back = [to_first(4)] + [pltpu.roll(x, 1, 1) for x in p]
            for c in range(chunks):
                here = at(k, c)
                dx = ahead(p_turn, c) - jnp.where(lane == 0, p_back[c], p_back[c + 1])
                east_out[here, :] = wet[here, :] * (east[here, :] + (spin_half * pole[here, :] - dx))

        def flux(i):
            k = b * BLOCK + i
            to_last, to_first = halo(i)
            u, w, t, q = ([f[at(k, c), :] for c in range(chunks)] for f in (east_out, wet, heat, salt))
            u_beyond = to_last(3) + to_last(2) * press[at(k, chunks - 1), :]
            u_turn, w_turn, t_turn, q_turn = (
                [pltpu.roll(x, last, 1) for x in f] + [beyond]
                for f, beyond in ((u, u_beyond), (w, to_last(2)), (t, to_last(0)), (q, to_last(1)))
            )
            w_out = to_first(2)
            u_out = to_first(3) - w_out * press[at(k, 0), :]
            out = fluxes(u_out, u[0], w_out * w[0], [(to_first(0), t[0]), (to_first(1), q[0])])
            for f in range(2):
                side_flux[spot(i, f, -1), :] = out[f]
            for c in range(chunks):
                out = fluxes(
                    u[c], ahead(u_turn, c), w[c] * ahead(w_turn, c), [(t[c], ahead(t_turn, c)), (q[c], ahead(q_turn, c))]
                )
                for f in range(2):
                    side_flux[spot(i, f, c), :] = out[f]

        def spot(i, f, c):
            return tile((i * 2 + f) * (chunks + 1) + c + 1)

        def gather(i):
            k = b * BLOCK + i
            x = [[side_flux[spot(i, f, c), :] for c in range(-1, chunks)] for f in range(2)]
            back = [[y[0]] + [pltpu.roll(z, 1, 1) for z in y[1:]] for y in x]
            for c in range(chunks):
                both = VERT * (wet[at(k, c), :] * wet[at(k + 1, c), :])
                for f, (field, out) in enumerate(((heat, heat_out), (salt, salt_out))):
                    q = field[at(k, c), :]
                    rise = both * (field[at(k + 1, c), :] - q)
                    held = slice((f * chunks + c) * ROWS, (f * chunks + c + 1) * ROWS)
                    gain = rise - upward[held, :]
                    upward[held, :] = rise
                    dx = x[f][c + 1] - jnp.where(lane == 0, back[f][c], back[f][c + 1])
                    out[at(k, c), :] = (q + gain) - dx

        for i in range(BLOCK + 2):
            if i < BLOCK:
                flow(i)
            if 0 < i <= BLOCK:
                flux(i - 1)
            if i > 1:
                gather(i - 2)
        return 0

    lax.fori_loop(0, blocks, second, 0)

    def third(b, _):
        for side in range(2):
            got = from_south if side == 0 else from_north

            @pl.when(has_below if side == 0 else has_above)
            def _():
                row_copy(b, 1 - side).wait_recv()

            for c in range(chunks):
                ch = slice(c * LANES, (c + 1) * LANES)
                q0, q1, w, part, p = (own_edge[own(b, side, f, c), :] for f in range(5))
                tracers = got[b, 0:16, ch].astype(jnp.float32)
                rest = got[b, 16:32, ch].astype(jnp.float32)
                far0, far1, w_far, v_far = tracers[0:8], tracers[8:16], rest[0:8], rest[8:16]
                d = w_far * (BUOY_SALT * far1 - BUOY_HEAT * far0)
                s = d
                for gap in (1, 2, 4):
                    s = s + jnp.where(row >= gap, pltpu.roll(s, gap, 0), 0.0)
                held = slice((side * chunks + c) * ROWS, (side * chunks + c + 1) * ROWS)
                s = s + tower[held, :]
                tower[held, :] = jnp.broadcast_to(s[BLOCK - 1 : BLOCK, :], (BLOCK, LANES))
                p_far = s - 0.5 * d
                if side == 0:
                    v = part + w * p_far
                    v_far = v_far - w_far * p
                    flux = fluxes(v_far, v, w * w_far, [(far0, q0), (far1, q1)])
                else:
                    v = part - w * p_far
                    v_far = v_far + w_far * p
                    flux = fluxes(v, v_far, w * w_far, [(q0, far0), (q1, far1)])
                for f, x in enumerate((v, *flux)):
                    edge_value[tile((side * 3 + f) * chunks + c), :] = x

        def level(i):
            k = b * BLOCK + i

            def edge(side, f, c):
                line = pl.ds(((side * 3 + f) * chunks + c) * ROWS + i, 1)
                return jnp.broadcast_to(edge_value[line, :], (ROWS, LANES))

            for c in range(chunks):
                here = at(k, c)
                p, w = press[here, :], wet[here, :]
                dy = pltpu.roll(p, ROWS - 1, 0) - pltpu.roll(p, 1, 0)
                v = w * (pole[here, :] - (spin_half * east[here, :] + dy))
                v = jnp.where(row == 0, edge(0, 0, c), jnp.where(row == ROWS - 1, edge(1, 0, c), v))
                pole_out[here, :] = v
                q = [heat[here, :], salt[here, :]]
                flux = fluxes(
                    v,
                    pltpu.roll(v, ROWS - 1, 0),
                    w * pltpu.roll(w, ROWS - 1, 0),
                    [(x, pltpu.roll(x, ROWS - 1, 0)) for x in q],
                )
                for f, out in enumerate((heat_out, salt_out)):
                    over = jnp.where(row == ROWS - 1, edge(1, f + 1, c), flux[f])
                    under = jnp.where(row == 0, edge(0, f + 1, c), pltpu.roll(flux[f], 1, 0))
                    out[here, :] = w * (out[here, :] - (over - under))

        several(level, AT_ONCE)

        groups = chunks // 4
        half = groups * 4 * ROWS
        for c in range(chunks):
            g, across = c // 4, slice((c % 4) * LANES, (c % 4 + 1) * LANES)
            for t, f in enumerate((heat_out, salt_out)):
                x = [f[at(b * BLOCK + i, c), :] for i in range(BLOCK)]
                add = [x[i] + x[BLOCK - 1 - i] for i in range(BLOCK // 2)]
                dif = [WAVE[i] * (x[i] - x[BLOCK - 1 - i]) for i in range(BLOCK // 2)]
                both = jnp.concatenate([FLAT * pairwise_sum(add), pairwise_sum(dif)], 0)
                high = both.astype(jnp.bfloat16)
                base = (g * 2 + t) * 2 * ROWS
                stack[base : base + 2 * ROWS, across] = high
                stack[half + base : half + base + 2 * ROWS, across] = (both - high.astype(jnp.float32)).astype(jnp.bfloat16)
        wide = jnp.dot(stack[...], lane_table[...], preferred_element_type=jnp.float32)
        short = (wide[:half, :LANES] + wide[half:, :LANES]) + (wide[:half, LANES:] + wide[half:, LANES:])
        for g in range(groups):
            for t in range(2):
                for p in range(2):
                    base = ((g * 2 + t) * 2 + p) * ROWS
                    z = short[base : base + ROWS, :]
                    flat, wave = FLAT * z, row_wave * z
                    z = jnp.where(row < 4, flat + pltpu.roll(flat, 4, 0), wave + pltpu.roll(wave, 4, 0))
                    z = z + pltpu.roll(z, 2, 0)
                    z = z + pltpu.roll(z, 1, 0)
                    z = jnp.where(row == 0, pltpu.roll(z, 5, 0), pltpu.roll(z, 2, 0))
                    coef_send[b, t, p, :, g * LANES : (g + 1) * LANES] = z[0:2, :].astype(jnp.bfloat16)
        for d in sorted(range(1, n_lon), key=lambda d: -min(d, n_lon - d)):
            coef_copy(b, d).start()
        coef_keep(b).start()
        return 0

    lax.fori_loop(0, blocks, third, 0)

    def settle(ref, sem):
        pltpu.make_async_copy(ref, ref, sem).wait()

    settle(coef_out.at[:, :, :, pl.ds(0, width * (n_lon - 1))], coef_sem)
    settle(coef_out.at[:, :, :, pl.ds(0, width * (n_lon - 1))], coef_send_sem)
    settle(coef_send, coef_keep_sem)
    settle(side_send.at[0], side_send_sem.at[0])
    settle(side_send.at[1], side_send_sem.at[1])

    @pl.when(has_below)
    def _():
        settle(row_send.at[0], row_send_sem.at[0])

    @pl.when(has_above)
    def _():
        settle(row_send.at[1], row_send_sem.at[1])


def deliver_kernel(pieces, *refs):
    count = len(refs) // 2
    sources, places, sem = refs[:count], refs[count : 2 * count], refs[-1]
    copies = []
    for i, (source, target) in enumerate(zip(sources, places)):
        parts = pieces if source.shape[0] % (8 * pieces) == 0 else 1
        size = source.shape[0] // parts
        for p in range(parts):
            part = pl.ds(p * size, size)
            copies.append(pltpu.make_async_copy(source.at[part], target.at[part], sem.at[i, p]))
    for copy in copies:
        copy.start()
    for copy in copies:
        copy.wait()


def deliver(arrays, pieces=1):
    return pl.pallas_call(
        functools.partial(deliver_kernel, pieces),
        out_shape=[pltpu.HBM(x.shape, x.dtype) for x in arrays],
        in_specs=[pl.BlockSpec(memory_space=pltpu.VMEM)] * len(arrays),
        out_specs=[pl.BlockSpec(memory_space=pl.ANY)] * len(arrays),
        scratch_shapes=[pltpu.SemaphoreType.DMA((len(arrays), pieces))],
        compiler_params=pltpu.CompilerParams(vmem_limit_bytes=1 << 20),
        name="deliver",
    )(*(pltpu.with_memory_space_constraint(x, pltpu.VMEM) for x in arrays))


def on_device(n_lat, n_lon, heat, salt, east, pole, spin, sea, depth):
    levels, rows, cols = heat.shape
    chunks, blocks = cols // LANES, levels // BLOCK
    tall = chunks * rows
    total = levels * tall
    field = pltpu.VMEM((total, LANES), jnp.float32)
    longer = pltpu.VMEM((total + tall, LANES), jnp.float32)
    dma = pltpu.SemaphoreType.DMA
    hbm = pl.BlockSpec(memory_space=pl.ANY)

    def tiled(x):
        x = x.reshape(x.shape[:-1] + (chunks, LANES))
        return jnp.swapaxes(x, -3, -2).reshape(-1, LANES)

    def whole(x):
        return jnp.swapaxes(x.reshape(levels, chunks, rows, LANES), 1, 2).reshape(levels, rows, cols)

    outs = pl.pallas_call(
        functools.partial(step_kernel, n_lat, n_lon),
        out_shape=[pltpu.VMEM((total, LANES), jnp.float32)] * 4
        + [pltpu.VMEM((2, 2 * blocks, 2, n_lon * cols // 4), jnp.bfloat16)],
        in_specs=[hbm] * 7,
        out_specs=[pl.BlockSpec(memory_space=pltpu.VMEM)] * 5,
        scratch_shapes=[
            longer,
            longer,
            field,
            field,
            pltpu.VMEM((total, LANES), jnp.int32),
            pltpu.VMEM((tall, LANES), jnp.int32),
            longer,
            field,
            pltpu.VMEM((2, blocks, 4 * BLOCK, cols), jnp.bfloat16),
            pltpu.VMEM((blocks, 4 * BLOCK, cols), jnp.bfloat16),
            pltpu.VMEM((blocks, 4 * BLOCK, cols), jnp.bfloat16),
            pltpu.VMEM((LANES, LANES), jnp.float32),
            pltpu.VMEM((2 * ROWS, LANES), jnp.float32),
            pltpu.VMEM((2, blocks, ROWS, LANES), jnp.float32),
            pltpu.VMEM((blocks, ROWS, LANES), jnp.float32),
            pltpu.VMEM((blocks, ROWS, LANES), jnp.float32),
            pltpu.VMEM((LANES, LANES), jnp.float32),
            pltpu.VMEM((LANES, LANES), jnp.float32),
            pltpu.VMEM((2 * tall, LANES), jnp.float32),
            pltpu.VMEM((BLOCK * 2 * (chunks + 1) * ROWS, LANES), jnp.float32),
            pltpu.VMEM((tall, LANES), jnp.float32),
            pltpu.VMEM((2 * tall, LANES), jnp.float32),
            pltpu.VMEM((blocks * 2 * 5 * tall, LANES), jnp.float32),
            pltpu.VMEM((2 * 3 * tall, LANES), jnp.float32),
            pltpu.VMEM((4 * LANES, 2 * LANES), jnp.bfloat16),
            pltpu.VMEM((chunks // 4 * 8 * ROWS, 4 * LANES), jnp.bfloat16),
            pltpu.VMEM((blocks, 2, 2, 2, cols // 4), jnp.bfloat16),
            pltpu.SMEM((rows,), jnp.float32),
            dma((blocks,)),
            dma,
            dma,
            dma((2,)),
            dma((blocks,)),
            dma((blocks,)),
            dma((2,)),
            dma((blocks,)),
            dma((blocks,)),
            dma,
            dma,
            dma,
        ],
        compiler_params=pltpu.CompilerParams(collective_id=0, has_side_effects=True, vmem_limit_bytes=28 << 20),
        name="ocean_step",
    )(
        *(
            pltpu.with_memory_space_constraint(x, pltpu.HBM)
            for x in (spin, tiled(heat), tiled(salt), tiled(east), tiled(pole), tiled(sea), tiled(depth))
        )
    )
    outs = deliver(outs)
    return tuple(whole(x) for x in outs[:4]) + (outs[4],)


def solution(mesh):
    field = P(None, "lat", "lon")
    return jax.shard_map(
        functools.partial(on_device, mesh.shape["lat"], mesh.shape["lon"]),
        mesh=mesh,
        in_specs=(field, field, field, field, P("lat"), field, P("lat", "lon")),
        out_specs=(field, field, field, field, P(None, None, "lat", None)),
        check_vma=False,
    )
```

```python
import functools
import math

import jax
import jax.numpy as jnp
from jax import lax
from jax.experimental import pallas as pl
from jax.experimental.pallas import tpu as pltpu
from jax.sharding import PartitionSpec as P

MESH = pl.DeviceIdType.MESH
BUOY_SALT = 0.25 * 0.25 * 0.8
BUOY_HEAT = 0.25 * 0.25 * 0.2
CARRY = 0.2 * 0.25
MIX = 0.2 * 0.8
VERT = 0.1
FLAT = math.sqrt(1.0 / 8.0)
WAVE = [math.sqrt(2.0 / 8.0) * math.cos(math.pi * (2 * n + 1) / 16.0) for n in range(8)]
ROWS = 8
LANES = 128
BLOCK = 8


def once(make):
    made = {}

    def get(c):
        if c not in made:
            made[c] = make(c)
        return made[c]

    return get


def pairwise_sum(parts):
    while len(parts) > 1:
        parts = [sum(parts[i : i + 2][1:], parts[i]) for i in range(0, len(parts), 2)]
    return parts[0]


def table_value(freq, place):
    wave = jnp.full(freq.shape, WAVE[0], jnp.float32)
    for n in range(1, 8):
        wave = jnp.where(place == n, WAVE[n], wave)
    return jnp.where(freq == 0, FLAT, wave)


def fluxes(near, far, both, pairs):
    t = CARRY * (near + far)
    a = both * (t + MIX)
    b = both * (t - MIX)
    return [a * q + b * n for q, n in pairs]


REVERSED = (0, 4, 2, 6, 1, 5, 3, 7)


AT_ONCE = 2


def several(level, count):
    def turn(i, _):
        for j in range(count):
            level(i * count + j)
        return 0

    lax.fori_loop(0, BLOCK // count, turn, 0)


def edge_rows(x, row):
    y = [x[i] for i in REVERSED]
    ends = (row == 0) | (row == ROWS - 1)
    outer = ends | (row == 3) | (row == 4)
    even = lax.rem(row, 2) == 0
    pairs = [jnp.where(ends, y[i], pltpu.roll(y[i + 1], 4, 0)) for i in range(0, 8, 2)]
    low, high = (jnp.where(outer, pairs[i], pltpu.roll(pairs[i + 1], 2, 0)) for i in (0, 2))
    high = pltpu.roll(high, 1, 0)
    return jnp.where(even, low, high), pltpu.roll(jnp.where(even, high, low), 1, 0)


def step_kernel(
    n_lat,
    n_lon,
    spin_hbm,
    heat_hbm,
    salt_hbm,
    east_hbm,
    pole_hbm,
    sea_hbm,
    depth_hbm,
    heat_out,
    salt_out,
    east_out,
    pole_out,
    coef_out,
    heat,
    salt,
    east,
    pole,
    sea,
    depth,
    wet,
    press,
    row_send,
    from_south,
    from_north,
    edge_box,
    turned_box,
    side_send,
    from_west,
    from_east,
    halo_box,
    halo_cols,
    upward,
    side_flux,
    below_sum,
    tower,
    own_edge,
    edge_value,
    lane_table,
    stack,
    coef_send,
    spin,
    load_sem,
    depth_sem,
    spin_sem,
    row_send_sem,
    south_sem,
    north_sem,
    side_send_sem,
    west_sem,
    east_sem,
    coef_send_sem,
    coef_sem,
    coef_keep_sem,
):
    chunks = depth.shape[0] // ROWS
    cols = chunks * LANES
    tall = chunks * ROWS
    total = press.shape[0]
    blocks = total // (tall * BLOCK)
    la = lax.axis_index("lat")
    lo = lax.axis_index("lon")
    above = {"lat": lax.rem(la + 1, n_lat)}
    below = {"lat": lax.rem(la + n_lat - 1, n_lat)}
    right = {"lon": lax.rem(lo + 1, n_lon)}
    left = {"lon": lax.rem(lo + n_lon - 1, n_lon)}
    has_above = la < n_lat - 1
    has_below = la > 0

    fields = ((heat_hbm, heat), (salt_hbm, salt), (sea_hbm, sea), (east_hbm, east), (pole_hbm, pole))

    def load(i, b):
        hbm, vmem = fields[i]
        part = pl.ds(pl.multiple_of(b * BLOCK * tall, BLOCK * tall), BLOCK * tall)
        return pltpu.make_async_copy(hbm.at[part], vmem.at[part], load_sem.at[b])

    barrier = pltpu.get_barrier_semaphore()
    peers = [above, below] + [{"lon": lax.rem(lo + d, n_lon)} for d in range(1, n_lon)]
    for peer in peers:
        pl.semaphore_signal(barrier, inc=1, device_id=peer, device_id_type=MESH)

    depth_load = pltpu.make_async_copy(depth_hbm, depth, depth_sem)
    depth_load.start()
    spin_load = pltpu.make_async_copy(spin_hbm, spin, spin_sem)
    spin_load.start()
    for b in range(blocks):
        for i in range(len(fields)):
            load(i, b).start()

    last = LANES - 1
    lane = lax.broadcasted_iota(jnp.int32, (ROWS, LANES), 1)
    row = lax.broadcasted_iota(jnp.int32, (ROWS, LANES), 0)
    zero = jnp.zeros((ROWS, LANES), jnp.float32)

    deep = lane_table.shape[0]
    n = lax.broadcasted_iota(jnp.int32, (deep, LANES), 0)
    o = lax.broadcasted_iota(jnp.int32, (deep, LANES), 1)
    table = jnp.where(n // 8 == o // 2, table_value(o % 2, n % 8), 0.0)
    high = table.astype(jnp.bfloat16)
    lane_table[:, :LANES] = high
    lane_table[:, LANES:] = (table - high.astype(jnp.float32)).astype(jnp.bfloat16)
    row_wave = table_value(jnp.ones_like(row), row)
    edge_box[...] = jnp.zeros_like(edge_box)
    halo_box[...] = jnp.zeros_like(halo_box)
    upward[...] = jnp.zeros_like(upward)
    below_sum[...] = jnp.zeros_like(below_sum)
    tower[...] = jnp.zeros_like(tower)
    for f in (heat, salt, wet):
        f[total:, :] = jnp.zeros((tall, LANES), jnp.float32)

    @pl.when(la == 0)
    def _():
        from_south[...] = jnp.zeros_like(from_south)

    @pl.when(la == n_lat - 1)
    def _():
        from_north[...] = jnp.zeros_like(from_north)

    spin_load.wait()
    spin_half = jnp.full((ROWS, LANES), 0.5 * spin[0], jnp.float32)
    for j in range(1, ROWS):
        spin_half = jnp.where(row == j, 0.5 * spin[j], spin_half)
    depth_load.wait()

    def at(k, c):
        return pl.ds(pl.multiple_of(k * tall, tall) + c * ROWS, ROWS)

    def tile(i):
        return pl.ds(pl.multiple_of(i * ROWS, ROWS), ROWS)

    def own(b, side, f, c):
        return tile(((b * 2 + side) * 5 + f) * chunks + c)

    def row_copy(b, side):
        return pltpu.make_async_remote_copy(
            src_ref=row_send.at[side, b],
            dst_ref=(from_north if side == 0 else from_south).at[b],
            send_sem=row_send_sem.at[side],
            recv_sem=(north_sem if side == 0 else south_sem).at[b],
            device_id=below if side == 0 else above,
            device_id_type=MESH,
        )

    def send_rows(b):
        @pl.when(has_below)
        def _():
            row_copy(b, 0).start()

        @pl.when(has_above)
        def _():
            row_copy(b, 1).start()

    def side_copy(b, side):
        return pltpu.make_async_remote_copy(
            src_ref=side_send.at[side, b],
            dst_ref=(from_east if side == 0 else from_west).at[b],
            send_sem=side_send_sem.at[side],
            recv_sem=(east_sem if side == 0 else west_sem).at[b],
            device_id=left if side == 0 else right,
            device_id_type=MESH,
        )

    width = cols // 4

    def place(owner):
        return pl.ds(pl.multiple_of(owner * width, LANES), width)

    def coef_copy(b, d):
        return pltpu.make_async_remote_copy(
            src_ref=coef_send.at[b],
            dst_ref=coef_out.at[:, pl.ds(2 * b, 2), :, place(lo)],
            send_sem=coef_send_sem,
            recv_sem=coef_sem,
            device_id={"lon": lax.rem(lo + d, n_lon)},
            device_id_type=MESH,
        )

    def coef_keep(b):
        here = coef_out.at[:, pl.ds(2 * b, 2), :, place(lo)]
        return pltpu.make_async_copy(coef_send.at[b], here, coef_keep_sem)

    def first(b, _):
        pltpu.make_async_copy(heat_hbm, heat.at[pl.ds(0, total)], load_sem.at[b]).wait()
        for c in range(chunks):
            deep = depth[c * ROWS : (c + 1) * ROWS, :]
            s = below_sum[c * ROWS : (c + 1) * ROWS, :]
            cells = []
            for i in range(BLOCK):
                k = b * BLOCK + i
                here = at(k, c)
                w = jnp.where(k < deep, sea[here, :], 0).astype(jnp.float32)
                t, q = heat[here, :], salt[here, :]
                d = w * (BUOY_SALT * q - BUOY_HEAT * t)
                s = s + d
                p = s - 0.5 * d
                wet[here, :] = w
                press[here, :] = p
                inner = jnp.where(row == 0, -pltpu.roll(p, ROWS - 1, 0), pltpu.roll(p, 1, 0))
                cells.append((t, q, w, w * ((pole[here, :] - spin_half * east[here, :]) + inner), p))
            below_sum[c * ROWS : (c + 1) * ROWS, :] = s
            edges = [edge_rows(x, row) for x in zip(*cells)]
            ch = slice(c * LANES, (c + 1) * LANES)
            for side in range(2):
                for f in range(5):
                    own_edge[own(b, side, f, c), :] = edges[f][side]
                for f in (0, 2):
                    pair = jnp.concatenate([edges[f][side], edges[f + 1][side]], 0)
                    row_send[side, b, 8 * f : 8 * f + 16, ch] = pair.astype(jnp.bfloat16)

        for i in range(BLOCK):
            k = b * BLOCK + i

            def ends(get):
                return jnp.where(lane == 0, get(at(k, 0)), get(at(k, chunks - 1)))

            p = [press[at(k, c), :] for c in (0, chunks - 1)]
            slope = jnp.where(lane == 0, -pltpu.roll(p[0], last, 1), pltpu.roll(p[1], 1, 1))
            w = ends(lambda x: wet[x, :])
            part = w * (ends(lambda x: east[x, :] + spin_half * pole[x, :]) + slope)
            box = zero
            values = (ends(lambda x: heat[x, :]), ends(lambda x: salt[x, :]), w, part, jnp.where(lane == 0, *p))
            for f, v in enumerate(values):
                box = jnp.where((lane == 2 * f) | (lane == 2 * f + 1), pltpu.roll(v, 2 * f + 1, 1), box)
            edge_box[i * ROWS : (i + 1) * ROWS, :] = box
        turned_box[...] = edge_box[...].T[: 2 * ROWS, :]
        for side in range(2):
            side_send[side, b] = turned_box[pl.ds(1 - side, ROWS, stride=2), :]
        @pl.when(b == 0)
        def _():
            pl.semaphore_wait(barrier, len(peers))

        side_copy(b, 0).start()
        side_copy(b, 1).start()

        @pl.when(b == 0)
        def _():
            send_rows(0)

        @pl.when(b == blocks - 2)
        def _():
            send_rows(1)

        return 0

    lax.fori_loop(0, blocks, first, 0)
    for b in range(2, blocks):
        send_rows(b)

    def second(b, _):
        side_copy(b, 0).wait_recv()
        side_copy(b, 1).wait_recv()
        halo_box[0:ROWS, :] = from_east[b]
        halo_box[ROWS : 2 * ROWS, :] = from_west[b]
        halo_cols[...] = halo_box[...].T

        def halo(i):
            beyond = halo_cols[tile(i), :]

            def to_last(f):
                return pltpu.roll(beyond, last - f, 1)

            def to_first(f):
                return pltpu.roll(beyond, LANES - ROWS - f, 1)

            return to_last, to_first

        def ahead(turned, c):
            return jnp.where(lane == last, turned[c + 1], turned[c])

        def flow(i):
            k = b * BLOCK + i
            to_last, to_first = halo(i)
            p = [press[at(k, c), :] for c in range(chunks)]
            p_turn = [pltpu.roll(x, last, 1) for x in p] + [to_last(4)]
            p_back = [to_first(4)] + [pltpu.roll(x, 1, 1) for x in p]
            for c in range(chunks):
                here = at(k, c)
                dx = ahead(p_turn, c) - jnp.where(lane == 0, p_back[c], p_back[c + 1])
                east_out[here, :] = wet[here, :] * (east[here, :] + (spin_half * pole[here, :] - dx))

        def flux(i):
            k = b * BLOCK + i
            to_last, to_first = halo(i)
            u, w, t, q = ([f[at(k, c), :] for c in range(chunks)] for f in (east_out, wet, heat, salt))
            u_beyond = to_last(3) + to_last(2) * press[at(k, chunks - 1), :]
            u_turn, w_turn, t_turn, q_turn = (
                [pltpu.roll(x, last, 1) for x in f] + [beyond]
                for f, beyond in ((u, u_beyond), (w, to_last(2)), (t, to_last(0)), (q, to_last(1)))
            )
            w_out = to_first(2)
            u_out = to_first(3) - w_out * press[at(k, 0), :]
            out = fluxes(u_out, u[0], w_out * w[0], [(to_first(0), t[0]), (to_first(1), q[0])])
            for f in range(2):
                side_flux[spot(i, f, -1), :] = out[f]
            for c in range(chunks):
                out = fluxes(
                    u[c], ahead(u_turn, c), w[c] * ahead(w_turn, c), [(t[c], ahead(t_turn, c)), (q[c], ahead(q_turn, c))]
                )
                for f in range(2):
                    side_flux[spot(i, f, c), :] = out[f]

        def spot(i, f, c):
            return tile((i * 2 + f) * (chunks + 1) + c + 1)

        def gather(i):
            k = b * BLOCK + i
            x = [[side_flux[spot(i, f, c), :] for c in range(-1, chunks)] for f in range(2)]
            back = [[y[0]] + [pltpu.roll(z, 1, 1) for z in y[1:]] for y in x]
            for c in range(chunks):
                both = VERT * (wet[at(k, c), :] * wet[at(k + 1, c), :])
                for f, (field, out) in enumerate(((heat, heat_out), (salt, salt_out))):
                    q = field[at(k, c), :]
                    rise = both * (field[at(k + 1, c), :] - q)
                    held = slice((f * chunks + c) * ROWS, (f * chunks + c + 1) * ROWS)
                    gain = rise - upward[held, :]
                    upward[held, :] = rise
                    dx = x[f][c + 1] - jnp.where(lane == 0, back[f][c], back[f][c + 1])
                    out[at(k, c), :] = (q + gain) - dx

        for i in range(BLOCK + 2):
            if i < BLOCK:
                flow(i)
            if 0 < i <= BLOCK:
                flux(i - 1)
            if i > 1:
                gather(i - 2)
        return 0

    lax.fori_loop(0, blocks, second, 0)

    along = range(2, n_lon, 2)
    crossing = range(1, n_lon, 2)

    def third(b, _):
        for side in range(2):
            got = from_south if side == 0 else from_north

            @pl.when(has_below if side == 0 else has_above)
            def _():
                row_copy(b, 1 - side).wait_recv()

            for c in range(chunks):
                ch = slice(c * LANES, (c + 1) * LANES)
                q0, q1, w, part, p = (own_edge[own(b, side, f, c), :] for f in range(5))
                tracers = got[b, 0:16, ch].astype(jnp.float32)
                rest = got[b, 16:32, ch].astype(jnp.float32)
                far0, far1, w_far, v_far = tracers[0:8], tracers[8:16], rest[0:8], rest[8:16]
                d = w_far * (BUOY_SALT * far1 - BUOY_HEAT * far0)
                s = d
                for gap in (1, 2, 4):
                    s = s + jnp.where(row >= gap, pltpu.roll(s, gap, 0), 0.0)
                held = slice((side * chunks + c) * ROWS, (side * chunks + c + 1) * ROWS)
                s = s + tower[held, :]
                tower[held, :] = jnp.broadcast_to(s[BLOCK - 1 : BLOCK, :], (BLOCK, LANES))
                p_far = s - 0.5 * d
                if side == 0:
                    v = part + w * p_far
                    v_far = v_far - w_far * p
                    flux = fluxes(v_far, v, w * w_far, [(far0, q0), (far1, q1)])
                else:
                    v = part - w * p_far
                    v_far = v_far + w_far * p
                    flux = fluxes(v, v_far, w * w_far, [(q0, far0), (q1, far1)])
                for f, x in enumerate((v, *flux)):
                    edge_value[tile((side * 3 + f) * chunks + c), :] = x

        @pl.when(b > 1)
        def _():
            for d in crossing:
                coef_copy(b - 2, d).start()

        @pl.when(b == blocks - 1)
        def _():
            for d in crossing:
                coef_copy(b - 1, d).start()

        def level(i):
            k = b * BLOCK + i

            def edge(side, f, c):
                line = pl.ds(((side * 3 + f) * chunks + c) * ROWS + i, 1)
                return jnp.broadcast_to(edge_value[line, :], (ROWS, LANES))

            for c in range(chunks):
                here = at(k, c)
                p, w = press[here, :], wet[here, :]
                dy = pltpu.roll(p, ROWS - 1, 0) - pltpu.roll(p, 1, 0)
                v = w * (pole[here, :] - (spin_half * east[here, :] + dy))
                v = jnp.where(row == 0, edge(0, 0, c), jnp.where(row == ROWS - 1, edge(1, 0, c), v))
                pole_out[here, :] = v
                q = [heat[here, :], salt[here, :]]
                flux = fluxes(
                    v,
                    pltpu.roll(v, ROWS - 1, 0),
                    w * pltpu.roll(w, ROWS - 1, 0),
                    [(x, pltpu.roll(x, ROWS - 1, 0)) for x in q],
                )
                for f, out in enumerate((heat_out, salt_out)):
                    over = jnp.where(row == ROWS - 1, edge(1, f + 1, c), flux[f])
                    under = jnp.where(row == 0, edge(0, f + 1, c), pltpu.roll(flux[f], 1, 0))
                    out[here, :] = w * (out[here, :] - (over - under))

        several(level, AT_ONCE)

        groups = chunks // 4
        half = groups * 4 * ROWS
        for c in range(chunks):
            g, across = c // 4, slice((c % 4) * LANES, (c % 4 + 1) * LANES)
            for t, f in enumerate((heat_out, salt_out)):
                x = [f[at(b * BLOCK + i, c), :] for i in range(BLOCK)]
                add = [x[i] + x[BLOCK - 1 - i] for i in range(BLOCK // 2)]
                dif = [WAVE[i] * (x[i] - x[BLOCK - 1 - i]) for i in range(BLOCK // 2)]
                both = jnp.concatenate([FLAT * pairwise_sum(add), pairwise_sum(dif)], 0)
                high = both.astype(jnp.bfloat16)
                base = (g * 2 + t) * 2 * ROWS
                stack[base : base + 2 * ROWS, across] = high
                stack[half + base : half + base + 2 * ROWS, across] = (both - high.astype(jnp.float32)).astype(jnp.bfloat16)
        wide = jnp.dot(stack[...], lane_table[...], preferred_element_type=jnp.float32)
        short = (wide[:half, :LANES] + wide[half:, :LANES]) + (wide[:half, LANES:] + wide[half:, LANES:])
        for g in range(groups):
            for t in range(2):
                for p in range(2):
                    base = ((g * 2 + t) * 2 + p) * ROWS
                    z = short[base : base + ROWS, :]
                    flat, wave = FLAT * z, row_wave * z
                    z = jnp.where(row < 4, flat + pltpu.roll(flat, 4, 0), wave + pltpu.roll(wave, 4, 0))
                    z = z + pltpu.roll(z, 2, 0)
                    z = z + pltpu.roll(z, 1, 0)
                    z = jnp.where(row == 0, pltpu.roll(z, 5, 0), pltpu.roll(z, 2, 0))
                    coef_send[b, t, p, :, g * LANES : (g + 1) * LANES] = z[0:2, :].astype(jnp.bfloat16)
        for d in along:
            coef_copy(b, d).start()

        @pl.when(b == blocks - 1)
        def _():
            for d in crossing:
                coef_copy(b, d).start()
        coef_keep(b).start()
        return 0

    lax.fori_loop(0, blocks, third, 0)

    def settle(ref, sem):
        pltpu.make_async_copy(ref, ref, sem).wait()

    settle(coef_out.at[:, :, :, pl.ds(0, width * (n_lon - 1))], coef_sem)
    settle(coef_out.at[:, :, :, pl.ds(0, width * (n_lon - 1))], coef_send_sem)
    settle(coef_send, coef_keep_sem)
    settle(side_send.at[0], side_send_sem.at[0])
    settle(side_send.at[1], side_send_sem.at[1])

    @pl.when(has_below)
    def _():
        settle(row_send.at[0], row_send_sem.at[0])

    @pl.when(has_above)
    def _():
        settle(row_send.at[1], row_send_sem.at[1])


def deliver_kernel(pieces, *refs):
    count = len(refs) // 2
    sources, places, sem = refs[:count], refs[count : 2 * count], refs[-1]
    copies = []
    for i, (source, target) in enumerate(zip(sources, places)):
        parts = pieces if source.shape[0] % (8 * pieces) == 0 else 1
        size = source.shape[0] // parts
        for p in range(parts):
            part = pl.ds(p * size, size)
            copies.append(pltpu.make_async_copy(source.at[part], target.at[part], sem.at[i, p]))
    for copy in copies:
        copy.start()
    for copy in copies:
        copy.wait()


def deliver(arrays, pieces=1):
    return pl.pallas_call(
        functools.partial(deliver_kernel, pieces),
        out_shape=[pltpu.HBM(x.shape, x.dtype) for x in arrays],
        in_specs=[pl.BlockSpec(memory_space=pltpu.VMEM)] * len(arrays),
        out_specs=[pl.BlockSpec(memory_space=pl.ANY)] * len(arrays),
        scratch_shapes=[pltpu.SemaphoreType.DMA((len(arrays), pieces))],
        compiler_params=pltpu.CompilerParams(vmem_limit_bytes=1 << 20),
        name="deliver",
    )(*(pltpu.with_memory_space_constraint(x, pltpu.VMEM) for x in arrays))


def on_device(n_lat, n_lon, heat, salt, east, pole, spin, sea, depth):
    levels, rows, cols = heat.shape
    chunks, blocks = cols // LANES, levels // BLOCK
    tall = chunks * rows
    total = levels * tall
    field = pltpu.VMEM((total, LANES), jnp.float32)
    longer = pltpu.VMEM((total + tall, LANES), jnp.float32)
    dma = pltpu.SemaphoreType.DMA
    hbm = pl.BlockSpec(memory_space=pl.ANY)

    def tiled(x):
        x = x.reshape(x.shape[:-1] + (chunks, LANES))
        return jnp.swapaxes(x, -3, -2).reshape(-1, LANES)

    def whole(x):
        return jnp.swapaxes(x.reshape(levels, chunks, rows, LANES), 1, 2).reshape(levels, rows, cols)

    outs = pl.pallas_call(
        functools.partial(step_kernel, n_lat, n_lon),
        out_shape=[pltpu.VMEM((total, LANES), jnp.float32)] * 4
        + [pltpu.VMEM((2, 2 * blocks, 2, n_lon * cols // 4), jnp.bfloat16)],
        in_specs=[hbm] * 7,
        out_specs=[pl.BlockSpec(memory_space=pltpu.VMEM)] * 5,
        scratch_shapes=[
            longer,
            longer,
            field,
            field,
            pltpu.VMEM((total, LANES), jnp.int32),
            pltpu.VMEM((tall, LANES), jnp.int32),
            longer,
            field,
            pltpu.VMEM((2, blocks, 4 * BLOCK, cols), jnp.bfloat16),
            pltpu.VMEM((blocks, 4 * BLOCK, cols), jnp.bfloat16),
            pltpu.VMEM((blocks, 4 * BLOCK, cols), jnp.bfloat16),
            pltpu.VMEM((LANES, LANES), jnp.float32),
            pltpu.VMEM((2 * ROWS, LANES), jnp.float32),
            pltpu.VMEM((2, blocks, ROWS, LANES), jnp.float32),
            pltpu.VMEM((blocks, ROWS, LANES), jnp.float32),
            pltpu.VMEM((blocks, ROWS, LANES), jnp.float32),
            pltpu.VMEM((LANES, LANES), jnp.float32),
            pltpu.VMEM((LANES, LANES), jnp.float32),
            pltpu.VMEM((2 * tall, LANES), jnp.float32),
            pltpu.VMEM((BLOCK * 2 * (chunks + 1) * ROWS, LANES), jnp.float32),
            pltpu.VMEM((tall, LANES), jnp.float32),
            pltpu.VMEM((2 * tall, LANES), jnp.float32),
            pltpu.VMEM((blocks * 2 * 5 * tall, LANES), jnp.float32),
            pltpu.VMEM((2 * 3 * tall, LANES), jnp.float32),
            pltpu.VMEM((4 * LANES, 2 * LANES), jnp.bfloat16),
            pltpu.VMEM((chunks // 4 * 8 * ROWS, 4 * LANES), jnp.bfloat16),
            pltpu.VMEM((blocks, 2, 2, 2, cols // 4), jnp.bfloat16),
            pltpu.SMEM((rows,), jnp.float32),
            dma((blocks,)),
            dma,
            dma,
            dma((2,)),
            dma((blocks,)),
            dma((blocks,)),
            dma((2,)),
            dma((blocks,)),
            dma((blocks,)),
            dma,
            dma,
            dma,
        ],
        compiler_params=pltpu.CompilerParams(collective_id=0, has_side_effects=True, vmem_limit_bytes=28 << 20),
        name="ocean_step",
    )(
        *(
            pltpu.with_memory_space_constraint(x, pltpu.HBM)
            for x in (spin, tiled(heat), tiled(salt), tiled(east), tiled(pole), tiled(sea), tiled(depth))
        )
    )
    outs = deliver(outs)
    return tuple(whole(x) for x in outs[:4]) + (outs[4],)


def solution(mesh):
    field = P(None, "lat", "lon")
    return jax.shard_map(
        functools.partial(on_device, mesh.shape["lat"], mesh.shape["lon"]),
        mesh=mesh,
        in_specs=(field, field, field, field, P("lat"), field, P("lat", "lon")),
        out_specs=(field, field, field, field, P(None, None, "lat", None)),
        check_vma=False,
    )
```

```python
import functools
import math

import jax
import jax.numpy as jnp
from jax import lax
from jax.experimental import pallas as pl
from jax.experimental.pallas import tpu as pltpu
from jax.sharding import PartitionSpec as P

MESH = pl.DeviceIdType.MESH
BUOY_SALT = 0.25 * 0.25 * 0.8
BUOY_HEAT = 0.25 * 0.25 * 0.2
CARRY = 0.2 * 0.25
MIX = 0.2 * 0.8
VERT = 0.1
FLAT = math.sqrt(1.0 / 8.0)
WAVE = [math.sqrt(2.0 / 8.0) * math.cos(math.pi * (2 * n + 1) / 16.0) for n in range(8)]
ROWS = 8
LANES = 128
BLOCK = 8


def once(make):
    made = {}

    def get(c):
        if c not in made:
            made[c] = make(c)
        return made[c]

    return get


def pairwise_sum(parts):
    while len(parts) > 1:
        parts = [sum(parts[i : i + 2][1:], parts[i]) for i in range(0, len(parts), 2)]
    return parts[0]


def table_value(freq, place):
    wave = jnp.full(freq.shape, WAVE[0], jnp.float32)
    for n in range(1, 8):
        wave = jnp.where(place == n, WAVE[n], wave)
    return jnp.where(freq == 0, FLAT, wave)


def fluxes(near, far, both, pairs):
    t = CARRY * (near + far)
    a = both * (t + MIX)
    b = both * (t - MIX)
    return [a * q + b * n for q, n in pairs]


REVERSED = (0, 4, 2, 6, 1, 5, 3, 7)


AT_ONCE = 8


def several(level, count):
    def turn(i, _):
        for j in range(count):
            level(i * count + j)
        return 0

    if count == BLOCK:
        turn(0, 0)
    else:
        lax.fori_loop(0, BLOCK // count, turn, 0)


def edge_rows(x, row):
    y = [x[i] for i in REVERSED]
    ends = (row == 0) | (row == ROWS - 1)
    outer = ends | (row == 3) | (row == 4)
    even = lax.rem(row, 2) == 0
    pairs = [jnp.where(ends, y[i], pltpu.roll(y[i + 1], 4, 0)) for i in range(0, 8, 2)]
    low, high = (jnp.where(outer, pairs[i], pltpu.roll(pairs[i + 1], 2, 0)) for i in (0, 2))
    high = pltpu.roll(high, 1, 0)
    return jnp.where(even, low, high), pltpu.roll(jnp.where(even, high, low), 1, 0)


def step_kernel(
    n_lat,
    n_lon,
    spin_hbm,
    heat_hbm,
    salt_hbm,
    east_hbm,
    pole_hbm,
    sea_hbm,
    depth_hbm,
    heat_out,
    salt_out,
    east_out,
    pole_out,
    coef_out,
    heat,
    salt,
    east,
    pole,
    sea,
    depth,
    wet,
    press,
    row_send,
    from_south,
    from_north,
    edge_box,
    turned_box,
    side_send,
    from_west,
    from_east,
    halo_box,
    halo_cols,
    upward,
    side_flux,
    below_sum,
    tower,
    own_edge,
    edge_value,
    lane_table,
    stack,
    coef_send,
    spin,
    load_sem,
    depth_sem,
    spin_sem,
    row_send_sem,
    south_sem,
    north_sem,
    side_send_sem,
    west_sem,
    east_sem,
    coef_send_sem,
    coef_sem,
    coef_keep_sem,
):
    chunks = depth.shape[0] // ROWS
    cols = chunks * LANES
    tall = chunks * ROWS
    total = press.shape[0]
    blocks = total // (tall * BLOCK)
    la = lax.axis_index("lat")
    lo = lax.axis_index("lon")
    above = {"lat": lax.rem(la + 1, n_lat)}
    below = {"lat": lax.rem(la + n_lat - 1, n_lat)}
    right = {"lon": lax.rem(lo + 1, n_lon)}
    left = {"lon": lax.rem(lo + n_lon - 1, n_lon)}
    has_above = la < n_lat - 1
    has_below = la > 0

    fields = ((heat_hbm, heat), (salt_hbm, salt), (sea_hbm, sea), (east_hbm, east), (pole_hbm, pole))

    def load(i, b):
        hbm, vmem = fields[i]
        part = pl.ds(pl.multiple_of(b * BLOCK * tall, BLOCK * tall), BLOCK * tall)
        return pltpu.make_async_copy(hbm.at[part], vmem.at[part], load_sem.at[b])

    barrier = pltpu.get_barrier_semaphore()
    peers = [above, below] + [{"lon": lax.rem(lo + d, n_lon)} for d in range(1, n_lon)]
    for peer in peers:
        pl.semaphore_signal(barrier, inc=1, device_id=peer, device_id_type=MESH)

    depth_load = pltpu.make_async_copy(depth_hbm, depth, depth_sem)
    depth_load.start()
    spin_load = pltpu.make_async_copy(spin_hbm, spin, spin_sem)
    spin_load.start()
    for b in range(blocks):
        for i in range(len(fields)):
            load(i, b).start()

    last = LANES - 1
    lane = lax.broadcasted_iota(jnp.int32, (ROWS, LANES), 1)
    row = lax.broadcasted_iota(jnp.int32, (ROWS, LANES), 0)
    zero = jnp.zeros((ROWS, LANES), jnp.float32)

    deep = lane_table.shape[0]
    n = lax.broadcasted_iota(jnp.int32, (deep, LANES), 0)
    o = lax.broadcasted_iota(jnp.int32, (deep, LANES), 1)
    table = jnp.where(n // 8 == o // 2, table_value(o % 2, n % 8), 0.0)
    high = table.astype(jnp.bfloat16)
    lane_table[:, :LANES] = high
    lane_table[:, LANES:] = (table - high.astype(jnp.float32)).astype(jnp.bfloat16)
    row_wave = table_value(jnp.ones_like(row), row)
    edge_box[...] = jnp.zeros_like(edge_box)
    halo_box[...] = jnp.zeros_like(halo_box)
    upward[...] = jnp.zeros_like(upward)
    below_sum[...] = jnp.zeros_like(below_sum)
    tower[...] = jnp.zeros_like(tower)
    for f in (heat, salt, wet):
        f[total:, :] = jnp.zeros((tall, LANES), jnp.float32)

    @pl.when(la == 0)
    def _():
        from_south[...] = jnp.zeros_like(from_south)

    @pl.when(la == n_lat - 1)
    def _():
        from_north[...] = jnp.zeros_like(from_north)

    spin_load.wait()
    spin_half = jnp.full((ROWS, LANES), 0.5 * spin[0], jnp.float32)
    for j in range(1, ROWS):
        spin_half = jnp.where(row == j, 0.5 * spin[j], spin_half)
    depth_load.wait()

    def at(k, c):
        return pl.ds(pl.multiple_of(k * tall, tall) + c * ROWS, ROWS)

    def tile(i):
        return pl.ds(pl.multiple_of(i * ROWS, ROWS), ROWS)

    def own(b, side, f, c):
        return tile(((b * 2 + side) * 5 + f) * chunks + c)

    def row_copy(b, side):
        return pltpu.make_async_remote_copy(
            src_ref=row_send.at[side, b],
            dst_ref=(from_north if side == 0 else from_south).at[b],
            send_sem=row_send_sem.at[side],
            recv_sem=(north_sem if side == 0 else south_sem).at[b],
            device_id=below if side == 0 else above,
            device_id_type=MESH,
        )

    def send_rows(b):
        @pl.when(has_below)
        def _():
            row_copy(b, 0).start()

        @pl.when(has_above)
        def _():
            row_copy(b, 1).start()

    def side_copy(b, side):
        return pltpu.make_async_remote_copy(
            src_ref=side_send.at[side, b],
            dst_ref=(from_east if side == 0 else from_west).at[b],
            send_sem=side_send_sem.at[side],
            recv_sem=(east_sem if side == 0 else west_sem).at[b],
            device_id=left if side == 0 else right,
            device_id_type=MESH,
        )

    width = cols // 4

    def place(owner):
        return pl.ds(pl.multiple_of(owner * width, LANES), width)

    def coef_copy(b, d):
        return pltpu.make_async_remote_copy(
            src_ref=coef_send.at[b],
            dst_ref=coef_out.at[:, pl.ds(2 * b, 2), :, place(lo)],
            send_sem=coef_send_sem,
            recv_sem=coef_sem,
            device_id={"lon": lax.rem(lo + d, n_lon)},
            device_id_type=MESH,
        )

    def coef_keep(b):
        here = coef_out.at[:, pl.ds(2 * b, 2), :, place(lo)]
        return pltpu.make_async_copy(coef_send.at[b], here, coef_keep_sem)

    def first(b, _):
        pltpu.make_async_copy(heat_hbm, heat.at[pl.ds(0, total)], load_sem.at[b]).wait()
        for c in range(chunks):
            deep = depth[c * ROWS : (c + 1) * ROWS, :]
            s = below_sum[c * ROWS : (c + 1) * ROWS, :]
            cells = []
            for i in range(BLOCK):
                k = b * BLOCK + i
                here = at(k, c)
                w = jnp.where(k < deep, sea[here, :], 0).astype(jnp.float32)
                t, q = heat[here, :], salt[here, :]
                d = w * (BUOY_SALT * q - BUOY_HEAT * t)
                s = s + d
                p = s - 0.5 * d
                wet[here, :] = w
                press[here, :] = p
                inner = jnp.where(row == 0, -pltpu.roll(p, ROWS - 1, 0), pltpu.roll(p, 1, 0))
                cells.append((t, q, w, w * ((pole[here, :] - spin_half * east[here, :]) + inner), p))
            below_sum[c * ROWS : (c + 1) * ROWS, :] = s
            edges = [edge_rows(x, row) for x in zip(*cells)]
            ch = slice(c * LANES, (c + 1) * LANES)
            for side in range(2):
                for f in range(5):
                    own_edge[own(b, side, f, c), :] = edges[f][side]
                for f in (0, 2):
                    pair = jnp.concatenate([edges[f][side], edges[f + 1][side]], 0)
                    row_send[side, b, 8 * f : 8 * f + 16, ch] = pair.astype(jnp.bfloat16)

        for i in range(BLOCK):
            k = b * BLOCK + i

            def ends(get):
                return jnp.where(lane == 0, get(at(k, 0)), get(at(k, chunks - 1)))

            p = [press[at(k, c), :] for c in (0, chunks - 1)]
            slope = jnp.where(lane == 0, -pltpu.roll(p[0], last, 1), pltpu.roll(p[1], 1, 1))
            w = ends(lambda x: wet[x, :])
            part = w * (ends(lambda x: east[x, :] + spin_half * pole[x, :]) + slope)
            box = zero
            values = (ends(lambda x: heat[x, :]), ends(lambda x: salt[x, :]), w, part, jnp.where(lane == 0, *p))
            for f, v in enumerate(values):
                box = jnp.where((lane == 2 * f) | (lane == 2 * f + 1), pltpu.roll(v, 2 * f + 1, 1), box)
            edge_box[i * ROWS : (i + 1) * ROWS, :] = box
        turned_box[...] = edge_box[...].T[: 3 * ROWS, :]
        for side in range(2):
            side_send[side, b] = turned_box[pl.ds(1 - side, ROWS, stride=2), :]
        @pl.when(b == 0)
        def _():
            pl.semaphore_wait(barrier, len(peers))

        side_copy(b, 0).start()
        side_copy(b, 1).start()

        @pl.when(b == 0)
        def _():
            send_rows(0)

        @pl.when(b == blocks - 2)
        def _():
            send_rows(1)

        return 0

    lax.fori_loop(0, blocks, first, 0)
    for b in range(2, blocks):
        send_rows(b)

    def second(b, _):
        side_copy(b, 0).wait_recv()
        side_copy(b, 1).wait_recv()
        halo_box[0:ROWS, :] = from_east[b]
        halo_box[ROWS : 2 * ROWS, :] = from_west[b]
        halo_cols[...] = halo_box[...].T

        def halo(i):
            beyond = halo_cols[tile(i), :]

            def to_last(f):
                return pltpu.roll(beyond, last - f, 1)

            def to_first(f):
                return pltpu.roll(beyond, LANES - ROWS - f, 1)

            return to_last, to_first

        def ahead(turned, c):
            return jnp.where(lane == last, turned[c + 1], turned[c])

        def flow(i):
            k = b * BLOCK + i
            to_last, to_first = halo(i)
            p = [press[at(k, c), :] for c in range(chunks)]
            p_turn = [pltpu.roll(x, last, 1) for x in p] + [to_last(4)]
            p_back = [to_first(4)] + [pltpu.roll(x, 1, 1) for x in p]
            for c in range(chunks):
                here = at(k, c)
                dx = ahead(p_turn, c) - jnp.where(lane == 0, p_back[c], p_back[c + 1])
                east_out[here, :] = wet[here, :] * (east[here, :] + (spin_half * pole[here, :] - dx))

        def flux(i):
            k = b * BLOCK + i
            to_last, to_first = halo(i)
            u, w, t, q = ([f[at(k, c), :] for c in range(chunks)] for f in (east_out, wet, heat, salt))
            u_beyond = to_last(3) + to_last(2) * press[at(k, chunks - 1), :]
            u_turn, w_turn, t_turn, q_turn = (
                [pltpu.roll(x, last, 1) for x in f] + [beyond]
                for f, beyond in ((u, u_beyond), (w, to_last(2)), (t, to_last(0)), (q, to_last(1)))
            )
            w_out = to_first(2)
            u_out = to_first(3) - w_out * press[at(k, 0), :]
            out = fluxes(u_out, u[0], w_out * w[0], [(to_first(0), t[0]), (to_first(1), q[0])])
            for f in range(2):
                side_flux[spot(i, f, -1), :] = out[f]
            for c in range(chunks):
                out = fluxes(
                    u[c], ahead(u_turn, c), w[c] * ahead(w_turn, c), [(t[c], ahead(t_turn, c)), (q[c], ahead(q_turn, c))]
                )
                for f in range(2):
                    side_flux[spot(i, f, c), :] = out[f]

        def spot(i, f, c):
            return tile((i * 2 + f) * (chunks + 1) + c + 1)

        def gather(i):
            k = b * BLOCK + i
            x = [[side_flux[spot(i, f, c), :] for c in range(-1, chunks)] for f in range(2)]
            back = [[y[0]] + [pltpu.roll(z, 1, 1) for z in y[1:]] for y in x]
            for c in range(chunks):
                both = VERT * (wet[at(k, c), :] * wet[at(k + 1, c), :])
                for f, (field, out) in enumerate(((heat, heat_out), (salt, salt_out))):
                    q = field[at(k, c), :]
                    rise = both * (field[at(k + 1, c), :] - q)
                    held = slice((f * chunks + c) * ROWS, (f * chunks + c + 1) * ROWS)
                    gain = rise - upward[held, :]
                    upward[held, :] = rise
                    dx = x[f][c + 1] - jnp.where(lane == 0, back[f][c], back[f][c + 1])
                    out[at(k, c), :] = (q + gain) - dx

        for i in range(BLOCK + 2):
            if i < BLOCK:
                flow(i)
            if 0 < i <= BLOCK:
                flux(i - 1)
            if i > 1:
                gather(i - 2)
        return 0

    lax.fori_loop(0, blocks, second, 0)

    along = range(2, n_lon, 2)
    crossing = range(1, n_lon, 2)

    def third(b, _):
        for side in range(2):
            got = from_south if side == 0 else from_north

            @pl.when(has_below if side == 0 else has_above)
            def _():
                row_copy(b, 1 - side).wait_recv()

            for c in range(chunks):
                ch = slice(c * LANES, (c + 1) * LANES)
                q0, q1, w, part, p = (own_edge[own(b, side, f, c), :] for f in range(5))
                tracers = got[b, 0:16, ch].astype(jnp.float32)
                rest = got[b, 16:32, ch].astype(jnp.float32)
                far0, far1, w_far, v_far = tracers[0:8], tracers[8:16], rest[0:8], rest[8:16]
                d = w_far * (BUOY_SALT * far1 - BUOY_HEAT * far0)
                s = d
                for gap in (1, 2, 4):
                    s = s + jnp.where(row >= gap, pltpu.roll(s, gap, 0), 0.0)
                held = slice((side * chunks + c) * ROWS, (side * chunks + c + 1) * ROWS)
                s = s + tower[held, :]
                tower[held, :] = jnp.broadcast_to(s[BLOCK - 1 : BLOCK, :], (BLOCK, LANES))
                p_far = s - 0.5 * d
                if side == 0:
                    v = part + w * p_far
                    v_far = v_far - w_far * p
                    flux = fluxes(v_far, v, w * w_far, [(far0, q0), (far1, q1)])
                else:
                    v = part - w * p_far
                    v_far = v_far + w_far * p
                    flux = fluxes(v, v_far, w * w_far, [(q0, far0), (q1, far1)])
                for f, x in enumerate((v, *flux)):
                    edge_value[tile((side * 3 + f) * chunks + c), :] = x

        @pl.when(b > 1)
        def _():
            for d in crossing:
                coef_copy(b - 2, d).start()

        @pl.when(b == blocks - 1)
        def _():
            for d in crossing:
                coef_copy(b - 1, d).start()

        def level(i):
            k = b * BLOCK + i

            def edge(side, f, c):
                line = pl.ds(((side * 3 + f) * chunks + c) * ROWS + i, 1)
                return jnp.broadcast_to(edge_value[line, :], (ROWS, LANES))

            for c in range(chunks):
                here = at(k, c)
                p, w = press[here, :], wet[here, :]
                dy = pltpu.roll(p, ROWS - 1, 0) - pltpu.roll(p, 1, 0)
                v = w * (pole[here, :] - (spin_half * east[here, :] + dy))
                v = jnp.where(row == 0, edge(0, 0, c), jnp.where(row == ROWS - 1, edge(1, 0, c), v))
                pole_out[here, :] = v
                q = [heat[here, :], salt[here, :]]
                flux = fluxes(
                    v,
                    pltpu.roll(v, ROWS - 1, 0),
                    w * pltpu.roll(w, ROWS - 1, 0),
                    [(x, pltpu.roll(x, ROWS - 1, 0)) for x in q],
                )
                for f, out in enumerate((heat_out, salt_out)):
                    over = jnp.where(row == ROWS - 1, edge(1, f + 1, c), flux[f])
                    under = jnp.where(row == 0, edge(0, f + 1, c), pltpu.roll(flux[f], 1, 0))
                    out[here, :] = w * (out[here, :] - (over - under))

        several(level, AT_ONCE)

        groups = chunks // 4
        half = groups * 4 * ROWS
        for c in range(chunks):
            g, across = c // 4, slice((c % 4) * LANES, (c % 4 + 1) * LANES)
            for t, f in enumerate((heat_out, salt_out)):
                x = [f[at(b * BLOCK + i, c), :] for i in range(BLOCK)]
                add = [x[i] + x[BLOCK - 1 - i] for i in range(BLOCK // 2)]
                dif = [WAVE[i] * (x[i] - x[BLOCK - 1 - i]) for i in range(BLOCK // 2)]
                both = jnp.concatenate([FLAT * pairwise_sum(add), pairwise_sum(dif)], 0)
                high = both.astype(jnp.bfloat16)
                base = (g * 2 + t) * 2 * ROWS
                stack[base : base + 2 * ROWS, across] = high
                stack[half + base : half + base + 2 * ROWS, across] = (both - high.astype(jnp.float32)).astype(jnp.bfloat16)
        wide = jnp.dot(stack[...], lane_table[...], preferred_element_type=jnp.float32)
        short = (wide[:half, :LANES] + wide[half:, :LANES]) + (wide[:half, LANES:] + wide[half:, LANES:])
        for g in range(groups):
            for t in range(2):
                for p in range(2):
                    base = ((g * 2 + t) * 2 + p) * ROWS
                    z = short[base : base + ROWS, :]
                    flat, wave = FLAT * z, row_wave * z
                    z = jnp.where(row < 4, flat + pltpu.roll(flat, 4, 0), wave + pltpu.roll(wave, 4, 0))
                    z = z + pltpu.roll(z, 2, 0)
                    z = z + pltpu.roll(z, 1, 0)
                    z = jnp.where(row == 0, pltpu.roll(z, 5, 0), pltpu.roll(z, 2, 0))
                    coef_send[b, t, p, :, g * LANES : (g + 1) * LANES] = z[0:2, :].astype(jnp.bfloat16)
        @pl.when(b == blocks - 1)
        def _():
            for d in sorted(crossing, key=lambda d: -min(d, n_lon - d)):
                coef_copy(b, d).start()

        for d in along:
            coef_copy(b, d).start()
        coef_keep(b).start()
        return 0

    lax.fori_loop(0, blocks, third, 0)

    def settle(ref, sem):
        pltpu.make_async_copy(ref, ref, sem).wait()

    settle(coef_out.at[:, :, :, pl.ds(0, width * (n_lon - 1))], coef_sem)
    settle(coef_out.at[:, :, :, pl.ds(0, width * (n_lon - 1))], coef_send_sem)
    settle(coef_send, coef_keep_sem)
    settle(side_send.at[0], side_send_sem.at[0])
    settle(side_send.at[1], side_send_sem.at[1])

    @pl.when(has_below)
    def _():
        settle(row_send.at[0], row_send_sem.at[0])

    @pl.when(has_above)
    def _():
        settle(row_send.at[1], row_send_sem.at[1])


def deliver_kernel(pieces, *refs):
    count = len(refs) // 2
    sources, places, sem = refs[:count], refs[count : 2 * count], refs[-1]
    copies = []
    for i, (source, target) in enumerate(zip(sources, places)):
        parts = pieces if source.shape[0] % (8 * pieces) == 0 else 1
        size = source.shape[0] // parts
        for p in range(parts):
            part = pl.ds(p * size, size)
            copies.append(pltpu.make_async_copy(source.at[part], target.at[part], sem.at[i, p]))
    for copy in copies:
        copy.start()
    for copy in copies:
        copy.wait()


def deliver(arrays, pieces=1):
    return pl.pallas_call(
        functools.partial(deliver_kernel, pieces),
        out_shape=[pltpu.HBM(x.shape, x.dtype) for x in arrays],
        in_specs=[pl.BlockSpec(memory_space=pltpu.VMEM)] * len(arrays),
        out_specs=[pl.BlockSpec(memory_space=pl.ANY)] * len(arrays),
        scratch_shapes=[pltpu.SemaphoreType.DMA((len(arrays), pieces))],
        compiler_params=pltpu.CompilerParams(vmem_limit_bytes=1 << 20),
        name="deliver",
    )(*(pltpu.with_memory_space_constraint(x, pltpu.VMEM) for x in arrays))


def on_device(n_lat, n_lon, heat, salt, east, pole, spin, sea, depth):
    levels, rows, cols = heat.shape
    chunks, blocks = cols // LANES, levels // BLOCK
    tall = chunks * rows
    total = levels * tall
    field = pltpu.VMEM((total, LANES), jnp.float32)
    longer = pltpu.VMEM((total + tall, LANES), jnp.float32)
    dma = pltpu.SemaphoreType.DMA
    hbm = pl.BlockSpec(memory_space=pl.ANY)

    def tiled(x):
        x = x.reshape(x.shape[:-1] + (chunks, LANES))
        return jnp.swapaxes(x, -3, -2).reshape(-1, LANES)

    def whole(x):
        return jnp.swapaxes(x.reshape(levels, chunks, rows, LANES), 1, 2).reshape(levels, rows, cols)

    outs = pl.pallas_call(
        functools.partial(step_kernel, n_lat, n_lon),
        out_shape=[pltpu.VMEM((total, LANES), jnp.float32)] * 4
        + [pltpu.VMEM((2, 2 * blocks, 2, n_lon * cols // 4), jnp.bfloat16)],
        in_specs=[hbm] * 7,
        out_specs=[pl.BlockSpec(memory_space=pltpu.VMEM)] * 5,
        scratch_shapes=[
            longer,
            longer,
            field,
            field,
            pltpu.VMEM((total, LANES), jnp.int32),
            pltpu.VMEM((tall, LANES), jnp.int32),
            longer,
            field,
            pltpu.VMEM((2, blocks, 4 * BLOCK, cols), jnp.bfloat16),
            pltpu.VMEM((blocks, 4 * BLOCK, cols), jnp.bfloat16),
            pltpu.VMEM((blocks, 4 * BLOCK, cols), jnp.bfloat16),
            pltpu.VMEM((LANES, LANES), jnp.float32),
            pltpu.VMEM((3 * ROWS, LANES), jnp.float32),
            pltpu.VMEM((2, blocks, ROWS, LANES), jnp.float32),
            pltpu.VMEM((blocks, ROWS, LANES), jnp.float32),
            pltpu.VMEM((blocks, ROWS, LANES), jnp.float32),
            pltpu.VMEM((LANES, LANES), jnp.float32),
            pltpu.VMEM((LANES, LANES), jnp.float32),
            pltpu.VMEM((2 * tall, LANES), jnp.float32),
            pltpu.VMEM((BLOCK * 2 * (chunks + 1) * ROWS, LANES), jnp.float32),
            pltpu.VMEM((tall, LANES), jnp.float32),
            pltpu.VMEM((2 * tall, LANES), jnp.float32),
            pltpu.VMEM((blocks * 2 * 5 * tall, LANES), jnp.float32),
            pltpu.VMEM((2 * 3 * tall, LANES), jnp.float32),
            pltpu.VMEM((4 * LANES, 2 * LANES), jnp.bfloat16),
            pltpu.VMEM((chunks // 4 * 8 * ROWS, 4 * LANES), jnp.bfloat16),
            pltpu.VMEM((blocks, 2, 2, 2, cols // 4), jnp.bfloat16),
            pltpu.SMEM((rows,), jnp.float32),
            dma((blocks,)),
            dma,
            dma,
            dma((2,)),
            dma((blocks,)),
            dma((blocks,)),
            dma((2,)),
            dma((blocks,)),
            dma((blocks,)),
            dma,
            dma,
            dma,
        ],
        compiler_params=pltpu.CompilerParams(collective_id=0, has_side_effects=True, vmem_limit_bytes=28 << 20),
        name="ocean_step",
    )(
        *(
            pltpu.with_memory_space_constraint(x, pltpu.HBM)
            for x in (spin, tiled(heat), tiled(salt), tiled(east), tiled(pole), tiled(sea), tiled(depth))
        )
    )
    outs = deliver(outs)
    return tuple(whole(x) for x in outs[:4]) + (outs[4],)


def solution(mesh):
    field = P(None, "lat", "lon")
    return jax.shard_map(
        functools.partial(on_device, mesh.shape["lat"], mesh.shape["lon"]),
        mesh=mesh,
        in_specs=(field, field, field, field, P("lat"), field, P("lat", "lon")),
        out_specs=(field, field, field, field, P(None, None, "lat", None)),
        check_vma=False,
    )
```
